32 devices in a mesh: dp: 4 (over y, x), block: 8 (over z, core).
Axes of the slice: x: 2, y: 2, z: 4, core: 2. Of those that a mesh axis runs over, the one named last changes fastest.
Arguments:
- positions: float32 [3, 8192], P(None, ('dp', 'block')), may hold values from -4 to 4
- neighbours: int32 [16, 8192], P(None, ('dp', 'block')), may hold values from 0 to 32
- atom_species: int32 [8192], P(('dp', 'block')), may hold values from 0 to 3
- tagged_atom: int32 [256], P(('dp', 'block')), may hold values from 0 to 31
- observed_in: int32 [256], P(('dp', 'block')), may hold values from 0 to 15
- targets: float32 [64], replicated, may hold values from -3 to 3
- noise_level: float32 [64], replicated, may hold values from 0.1 to 1
- embed_scale: float32 [4, 128], replicated, may hold values from -4 to 4
- embed_shift: float32 [4, 128], replicated, may hold values from -3 to 3
- first_weight: float32 [128, 256], replicated, may hold values from -1.5 to 1.5
- first_bias: float32 [256], replicated, may hold values from -3 to 3
- middle_weight: float32 [256, 256], replicated, may hold values from -0.375 to 0.375
- middle_bias: float32 [256], replicated, may hold values from -3 to 3
- energy_weight: float32 [4, 256], replicated, may hold values from -0.375 to 0.375
- covariance: float32 [8, 2048, 2048], P('block', 'dp'), as said below
Outputs:
- new_weights: float32 [8, 2048], P('block', 'dp')
- new_covariance: float32 [8, 2048, 2048], P('block', 'dp')
The draws below stay inside these ranges and needn't reach their ends.
Inputs may be any that keep to these rules, and one draw needn't show every extreme that they name: `neighbours`: a value of 32 marks an empty slot; any other value counts an atom of the same structure. `tagged_atom`: counted within the structure. `observed_in`: the observation is counted within the structure's group. `covariance`: every block is symmetric and positive definite.
All inputs are finite; a program needn't handle non-finite values.
Results may differ from the reference program's by a relative error of at most 0.0003.
Values sent between devices are 32-bit elements; how exact they have to be, the bound alone decides.
A program may use at most 64 MiB of HBM per device.

```python
import math
import jax
import jax.numpy as jnp
import numpy as np
from jax import lax

ORDER = 2048
HID = 256
EMB = 128
SPECIES = 4
NNEI = 16
ATOMS_STR = 32
OBS = 64
OBS_DP = 16
WROWS = 64
STRUCTS = 256
ATOMS = 8192
N_DP = 4
N_BLOCK = 8


def draw_covariance(key, part):
    first_key = jax.random.fold_in(key, 11)
    second_key = jax.random.fold_in(key, 12)
    entries = jax.random.normal(first_key, (N_BLOCK, ORDER, ORDER), jnp.float32)
    symmetric = (entries + jnp.swapaxes(entries, 1, 2)) * (0.45 / math.sqrt(ORDER))
    diagonal = jax.random.uniform(second_key, (N_BLOCK, ORDER), jnp.float32, 2.0, 3.0)
    return symmetric + diagonal[:, :, None] * jnp.eye(ORDER, dtype=jnp.float32)[None]


def set_ends(array, key, smallest, largest):
    place = [jax.random.randint(jax.random.fold_in(key, axis), (), 0, length) for axis, length in enumerate(array.shape)]
    widest = array.shape.index(max(array.shape))
    neighbour = place[:widest] + [(place[widest] + 1) % array.shape[widest]] + place[widest + 1:]
    return array.at[tuple(place)].set(smallest).at[tuple(neighbour)].set(largest)


def block_scale(key, extent, pieces, low, largest):
    def one(position, parts):
        heights = jax.random.uniform(jax.random.fold_in(jax.random.fold_in(key, 6), position), (parts,), jnp.float32, low / len(pieces), largest / len(pieces))
        return jnp.repeat(jnp.exp(heights), extent[position] // parts).reshape((-1,) + (1,) * (len(extent) - position - 1))

    loudness = one(*pieces[0])
    for cut in pieces[1:]:
        loudness = loudness * one(*cut)
    return loudness


def bell_draw(stream_key, extent, deviation, reach, pieces=(), held_as=jnp.bfloat16):
    values = deviation * jax.random.normal(stream_key, extent, jnp.float32)
    if pieces:
        values = values * block_scale(stream_key, extent, pieces, -0.22, 0.18)
    return jnp.clip(values, -reach, reach).astype(held_as)


def setup_inputs(seed: int = 0) -> dict:
    streams_of = jax.random.split(jax.random.key(seed), 16)
    positions = bell_draw(streams_of[0], (3, ATOMS), 1.0, 4.0, ((1, 32),), jnp.float32)
    neighbours = set_ends(jax.random.randint(streams_of[1], (NNEI, ATOMS), 0, ATOMS_STR + 1), jax.random.fold_in(streams_of[1], 1), 0, ATOMS_STR).astype(jnp.int32)
    atom_species = set_ends(jax.random.randint(streams_of[2], (ATOMS,), 0, SPECIES), jax.random.fold_in(streams_of[2], 1), 0, SPECIES - 1).astype(jnp.int32)
    tagged_atom = set_ends(jax.random.randint(streams_of[3], (STRUCTS,), 0, ATOMS_STR), jax.random.fold_in(streams_of[3], 1), 0, ATOMS_STR - 1).astype(jnp.int32)
    observed_in = set_ends(jax.random.randint(streams_of[4], (STRUCTS,), 0, OBS_DP), jax.random.fold_in(streams_of[4], 1), 0, OBS_DP - 1).astype(jnp.int32)
    targets = bell_draw(streams_of[5], (OBS,), 0.5, 3.0, (), jnp.float32)
    noise_level = jnp.clip(jnp.exp(jax.random.uniform(streams_of[6], (OBS,), jnp.float32, math.log(0.1), math.log(1.0))), 0.1, 1.0)
    embed_scale = bell_draw(streams_of[7], (SPECIES, EMB), 1.0, 4.0, (), jnp.float32)
    embed_shift = bell_draw(streams_of[8], (SPECIES, EMB), 0.5, 3.0, (), jnp.float32)
    first_weight = bell_draw(streams_of[9], (EMB, HID), (EMB // 8) ** -0.5, 1.5, (), jnp.float32)
    first_bias = bell_draw(streams_of[10], (HID,), 0.5, 3.0, (), jnp.float32)
    middle_weight = bell_draw(streams_of[11], (HID, HID), HID ** -0.5, 0.375, (), jnp.float32)
    middle_bias = bell_draw(streams_of[12], (HID,), 0.5, 3.0, (), jnp.float32)
    energy_weight = bell_draw(streams_of[13], (SPECIES, HID), HID ** -0.5, 0.375, (), jnp.float32)
    covariance = draw_covariance(jax.random.fold_in(streams_of[15], 71), 0)
    return dict(positions=positions, neighbours=neighbours, atom_species=atom_species, tagged_atom=tagged_atom, observed_in=observed_in, targets=targets, noise_level=noise_level, embed_scale=embed_scale, embed_shift=embed_shift, first_weight=first_weight, first_bias=first_bias, middle_weight=middle_weight, middle_bias=middle_bias, energy_weight=energy_weight, covariance=covariance)


radial_width = 4.0
forgetting = 0.98
highest = lax.Precision.HIGHEST

def observations(window, positions, neighbours, atom_species, tagged_atom, observed_in, embed_scale, embed_shift, first_weight, first_bias, middle_weight, middle_bias, energy_weight, obs_count, weighting):
    atom_total = positions.shape[1]
    struct_total = tagged_atom.shape[0]
    struct_size = atom_total // struct_total
    species_count = embed_scale.shape[0]
    slot_count = neighbours.shape[0]
    struct_start = jnp.arange(atom_total, dtype=jnp.int32) // struct_size * struct_size
    live_slot = (neighbours < struct_size).astype(jnp.float32)
    neighbour_at = struct_start[None, :] + jnp.minimum(neighbours, struct_size - 1)
    near_species = atom_species[neighbour_at]
    species_range = jnp.arange(species_count, dtype=jnp.int32)
    species_table = (near_species[None, :, :] == species_range[:, None, None]).astype(jnp.float32)
    edge_scale = jnp.einsum('se,ska->eka', embed_scale, species_table, precision=highest)
    edge_shift = jnp.einsum('se,ska->eka', embed_shift, species_table, precision=highest)
    own_species = (atom_species[None, :] == species_range[:, None]).astype(jnp.float32)
    readout = jnp.dot(energy_weight.T, own_species, precision=highest)
    remainder = middle_weight[window.shape[0]:]

    def site_energy(coords, middle):
        displace = coords[:, neighbour_at] - coords[:, None, :]
        distance_sq = lax.optimization_barrier(jnp.sum(displace * displace, axis=0))
        radial = jnp.exp(-distance_sq / radial_width) * live_slot
        embedded = jnp.tanh(radial[None] * edge_scale + edge_shift)
        descriptor = lax.optimization_barrier(jnp.sum(radial[None] * embedded, axis=1)) / slot_count
        first_layer = jnp.tanh(jnp.dot(first_weight.T, descriptor, precision=highest) + first_bias[:, None])
        second_layer = jnp.tanh(jnp.dot(middle.T, first_layer, precision=highest) + middle_bias[:, None])
        return lax.optimization_barrier(jnp.sum(readout * second_layer, axis=0))

    def predict(window_part):
        middle = jnp.concatenate([window_part, remainder], axis=0)
        energies, pullback = jax.vjp(lambda coords: site_energy(coords, middle), positions)
        forces = -pullback(jnp.ones_like(energies))[0]
        per_struct = lax.optimization_barrier(jnp.sum(energies.reshape(struct_total, struct_size), axis=1)) / struct_size
        tag_table = (tagged_atom[:, None] == jnp.arange(struct_size, dtype=jnp.int32)[None, :]).astype(jnp.float32)
        picked = lax.optimization_barrier(jnp.sum(forces.reshape(3, struct_total, struct_size) * tag_table[None], axis=2))
        values = jnp.concatenate([per_struct[None, :], picked], axis=0)
        value_rows = values[np.arange(obs_count) % 4]
        chosen = (observed_in[None, :] == jnp.arange(obs_count, dtype=jnp.int32)[:, None]).astype(jnp.float32)
        return lax.optimization_barrier(jnp.sum(chosen * value_rows, axis=1)) * weighting
    predicted, pullback = jax.vjp(predict, window)
    basis = jnp.eye(obs_count, dtype=predicted.dtype)
    jacobian = lax.map(lambda row: pullback(row)[0], basis)
    return (predicted, jacobian)

def reference(positions, neighbours, atom_species, tagged_atom, observed_in, targets, noise_level, embed_scale, embed_shift, first_weight, first_bias, middle_weight, middle_bias, energy_weight, covariance):
    device_total = N_DP * N_BLOCK
    per_device = positions.shape[1] // device_total
    struct_device = tagged_atom.shape[0] // device_total
    window = middle_weight[:WROWS]
    weighting = OBS / tagged_atom.shape[0]
    coords_all = positions.reshape(3, N_DP, N_BLOCK, per_device).transpose(1, 2, 0, 3)
    lists_all = neighbours.reshape(NNEI, N_DP, N_BLOCK, per_device).transpose(1, 2, 0, 3)
    species_all = atom_species.reshape(N_DP, N_BLOCK, per_device)
    tagged_all = tagged_atom.reshape(N_DP, N_BLOCK, struct_device)
    observed_all = observed_in.reshape(N_DP, N_BLOCK, struct_device)

    def one_group(group_inputs):

        def one_device(carry, device_inputs):
            coords, lists, species, tagged, observed = device_inputs
            predicted, jacobian = observations(window, coords, lists, species, tagged, observed, embed_scale, embed_shift, first_weight, first_bias, middle_weight, middle_bias, energy_weight, OBS_DP, weighting)
            return ((carry[0] + predicted, carry[1] + jacobian), None)
        initial = (jnp.zeros((OBS_DP,), positions.dtype), jnp.zeros((OBS_DP, WROWS, HID), positions.dtype))
        return lax.scan(one_device, initial, group_inputs)[0]
    predicted, jacobian = lax.map(one_group, (coords_all, lists_all, species_all, tagged_all, observed_all))
    predicted = predicted.reshape(OBS)
    jacobian = jacobian.reshape(OBS, N_BLOCK, ORDER)
    product = jnp.einsum('bij,obj->bio', covariance, jacobian, precision=highest)
    gram_sum = jnp.einsum('obi,bip->op', jacobian, product, precision=highest)
    gram_sum = 0.5 * (gram_sum + gram_sum.T) + jnp.diag(noise_level)
    factor = jnp.linalg.cholesky(gram_sum)
    inverse = jax.scipy.linalg.cho_solve((factor, True), jnp.eye(OBS, dtype=gram_sum.dtype))
    gain = jnp.einsum('bio,op->bip', product, inverse, precision=highest)
    innovation = targets - predicted
    new_weights = window.reshape(N_BLOCK, ORDER) + jnp.einsum('bio,o->bi', gain, innovation, precision=highest)
    new_covariance = (covariance - jnp.einsum('bio,bjo->bij', gain, product, precision=highest)) / forgetting
    return (new_weights, new_covariance)
```

```python
import functools

import jax
import jax.numpy as jnp
from jax import lax
from jax.experimental import pallas as pl
from jax.experimental.pallas import tpu as pltpu
from jax.sharding import PartitionSpec as P

OBS = 64
AUX = 128

radial_width = 4.0
forgetting = 0.98
highest = lax.Precision.HIGHEST


def contract(left, right, left_dim, right_dim):
    return lax.dot_general(
        left,
        right,
        (((left_dim,), (right_dim,)), ((), ())),
        precision=highest,
        preferred_element_type=jnp.float32,
    )


def observe_kernel(
    weighting,
    tagged_ref,
    observed_ref,
    positions_ref,
    neighbours_ref,
    species_ref,
    scale_ref,
    shift_ref,
    first_weight_ref,
    first_bias_ref,
    middle_ref,
    middle_bias_ref,
    energy_ref,
    out_ref,
    radial_ref,
    slope_ref,
    near_ref,
    scale_cols,
    shift_cols,
    desc_ref,
):
    atoms = positions_ref.shape[1]
    structs = tagged_ref.shape[1]
    struct_size = atoms // structs
    slots = neighbours_ref.shape[0]
    species_count, channels = scale_ref.shape
    hidden = middle_ref.shape[1]
    blocks = out_ref.shape[0]
    order = out_ref.shape[2] - AUX
    block_rows = order // hidden
    rows = blocks * block_rows

    lane = lax.broadcasted_iota(jnp.int32, (1, atoms), 1)
    start = jnp.zeros_like(lane)
    tag = jnp.zeros_like(lane)
    comp = jnp.zeros_like(lane)
    for s in range(structs):
        here = jnp.logical_and(lane >= s * struct_size, lane < (s + 1) * struct_size)
        start = jnp.where(here, s * struct_size, start)
        tag = jnp.where(here, tagged_ref[0, s], tag)
        comp = jnp.where(here, observed_ref[0, s] & 3, comp)
    inside = lane - start
    own = species_ref[...]

    for base in range(0, atoms, 128):
        cols = slice(base, base + 128)
        listed = neighbours_ref[:, cols]
        near = jnp.minimum(listed, struct_size - 1)
        index = near + (start[:, cols] - base)

        def pick(row):
            wide = jnp.broadcast_to(row, (slots, 128))
            return jnp.take_along_axis(wide, index, axis=1, mode="promise_in_bounds")

        shift_by = []
        for axis in range(3):
            mine = positions_ref[axis : axis + 1, cols]
            shift_by.append(pick(mine) - mine)
        distance_sq = shift_by[0] * shift_by[0]
        for axis in range(1, 3):
            distance_sq = distance_sq + shift_by[axis] * shift_by[axis]
        live = listed < struct_size
        radial = jnp.where(live, jnp.exp(-distance_sq / radial_width), 0.0)
        near_species = pick(own[:, cols].astype(jnp.float32))
        kind = comp[:, cols]
        along = jnp.where(kind == 1, shift_by[0], 0.0)
        along = jnp.where(kind == 2, shift_by[1], along)
        along = jnp.where(kind == 3, shift_by[2], along)
        moved = (near == tag[:, cols]).astype(jnp.float32) - (
            inside[:, cols] == tag[:, cols]
        ).astype(jnp.float32)
        slope = (-2.0 / radial_width) * radial * along * moved
        for k in range(slots):
            radial_ref[k, :, cols] = jnp.broadcast_to(radial[k : k + 1], (8, 128))
            slope_ref[k, :, cols] = jnp.broadcast_to(slope[k : k + 1], (8, 128))
            near_ref[k, :, cols] = jnp.broadcast_to(near_species[k : k + 1], (8, 128))

    scale_t = scale_ref[...].T
    shift_t = shift_ref[...].T
    for i in range(species_count):
        scale_cols[i] = jnp.broadcast_to(scale_t[:, i : i + 1], (channels, 128))
        shift_cols[i] = jnp.broadcast_to(shift_t[:, i : i + 1], (channels, 128))

    def embed(group, _):
        group_rows = pl.ds(pl.multiple_of(group * 8, 8), 8)
        scales = [scale_cols[i, group_rows, :] for i in range(species_count)]
        shifts = [shift_cols[i, group_rows, :] for i in range(species_count)]
        for base in range(0, atoms, 128):
            cols = slice(base, base + 128)
            total = jnp.zeros((8, 128), jnp.float32)
            moved = jnp.zeros((8, 128), jnp.float32)
            for k in range(slots):
                radial = radial_ref[k, :, cols]
                slope = slope_ref[k, :, cols]
                near = near_ref[k, :, cols]
                scale, shift = scales[-1], shifts[-1]
                for i in range(species_count - 1):
                    same = near == float(i)
                    scale = jnp.where(same, scales[i], scale)
                    shift = jnp.where(same, shifts[i], shift)
                scaled = radial * scale
                bent = jnp.tanh(scaled + shift)
                total = total + radial * bent
                moved = moved + slope * (bent + scaled * (1.0 - bent * bent))
            desc_ref[group_rows, cols] = total * (1.0 / slots)
            desc_ref[group_rows, slice(atoms + base, atoms + base + 128)] = moved * (
                1.0 / slots
            )
        return 0

    lax.fori_loop(0, channels // 8, embed, 0)

    first_bias = jnp.broadcast_to(first_bias_ref[...], (8, hidden)).T[:, :1]
    middle_bias = jnp.broadcast_to(middle_bias_ref[...], (8, hidden)).T[:, :1]
    energy_t = energy_ref[...].T
    lower = contract(first_weight_ref[...], desc_ref[...], 0, 0)
    first = jnp.tanh(lower[:, :atoms] + first_bias)
    first_moved = (1.0 - first * first) * lower[:, atoms:]
    upper = contract(middle_ref[...], jnp.concatenate([first, first_moved], axis=1), 0, 0)
    second = jnp.tanh(upper[:, :atoms] + middle_bias)
    moved = upper[:, atoms:]
    readout = jnp.broadcast_to(
        energy_t[:, species_count - 1 : species_count], (hidden, atoms)
    )
    for i in range(species_count - 1):
        readout = jnp.where(own == i, energy_t[:, i : i + 1], readout)
    gate = readout * (1.0 - second * second)
    mean = jnp.where(comp == 0, 1.0 / struct_size, 0.0)
    value = mean * jnp.sum(readout * second, axis=0, keepdims=True) - jnp.sum(
        gate * moved, axis=0, keepdims=True
    )
    bend = 2.0 * second * gate * moved + mean * gate

    struct_row = lax.broadcasted_iota(jnp.int32, (structs, atoms), 0)
    member = jnp.where(start == struct_row * struct_size, weighting, 0.0)
    struct_value = jnp.sum(member * value, axis=1, keepdims=True)
    left = jnp.concatenate([-first_moved[:rows], first[:rows]], axis=1)
    right = jnp.concatenate([gate, bend], axis=1)
    member_twice = jnp.concatenate([member, member], axis=1)
    spread = (left[:, None, :] * member_twice[None]).reshape(rows * structs, 2 * atoms)
    terms = contract(spread, right, 1, 1)
    for h in range(rows):
        place = (h % block_rows) * hidden
        out_ref[h // block_rows, :, place : place + hidden] = terms[
            h * structs : (h + 1) * structs
        ]
    row = lax.broadcasted_iota(jnp.int32, (structs, AUX), 0)
    column = lax.broadcasted_iota(jnp.int32, (structs, AUX), 1)
    observed = jnp.zeros((structs, AUX), jnp.int32)
    for s in range(structs):
        observed = jnp.where(row == s, observed_ref[0, s], observed)
    aux = jnp.where(
        column < OBS, (observed == column).astype(jnp.float32), struct_value
    )
    for b in range(blocks):
        out_ref[b, :, order:] = aux


def observe(
    blocks,
    order,
    weighting,
    positions,
    neighbours,
    atom_species,
    tagged_atom,
    observed_in,
    embed_scale,
    embed_shift,
    first_weight,
    first_bias,
    middle_weight,
    middle_bias,
    energy_weight,
):
    atoms = positions.shape[1]
    structs = tagged_atom.shape[0]
    slots = neighbours.shape[0]
    species_count, channels = embed_scale.shape
    vmem = pl.BlockSpec(memory_space=pltpu.VMEM)
    smem = pl.BlockSpec(memory_space=pltpu.SMEM)
    return pl.pallas_call(
        functools.partial(observe_kernel, weighting),
        out_shape=jax.ShapeDtypeStruct((blocks, structs, order + AUX), jnp.float32),
        in_specs=[smem, smem] + [vmem] * 10,
        out_specs=vmem,
        scratch_shapes=[
            pltpu.VMEM((slots, 8, atoms), jnp.float32),
            pltpu.VMEM((slots, 8, atoms), jnp.float32),
            pltpu.VMEM((slots, 8, atoms), jnp.float32),
            pltpu.VMEM((species_count, channels, 128), jnp.float32),
            pltpu.VMEM((species_count, channels, 128), jnp.float32),
            pltpu.VMEM((channels, 2 * atoms), jnp.float32),
        ],
    )(
        tagged_atom[None],
        observed_in[None],
        positions,
        neighbours,
        atom_species[None],
        embed_scale,
        embed_shift,
        first_weight,
        first_bias[None],
        middle_weight,
        middle_bias[None],
        energy_weight,
    )


def local(
    positions,
    neighbours,
    atom_species,
    tagged_atom,
    observed_in,
    targets,
    noise_level,
    embed_scale,
    embed_shift,
    first_weight,
    first_bias,
    middle_weight,
    middle_bias,
    energy_weight,
    covariance,
):
    group_count = lax.axis_size("dp")
    block_count = lax.axis_size("block")
    block_order = covariance.shape[2]
    row_share = covariance.shape[1]
    hidden = middle_weight.shape[1]
    block_rows = block_order // hidden
    window = middle_weight[: block_rows * block_count]
    obs_group = OBS // group_count
    weighting = OBS / (tagged_atom.shape[0] * group_count * block_count)
    terms = observe(
        block_count,
        block_order,
        weighting,
        positions,
        neighbours,
        atom_species,
        tagged_atom,
        observed_in,
        embed_scale,
        embed_shift,
        first_weight,
        first_bias,
        middle_weight,
        middle_bias,
        energy_weight,
    )
    chosen = (
        observed_in[:, None] == jnp.arange(obs_group, dtype=jnp.int32)[None, :]
    ).astype(jnp.float32)
    by_obs = jnp.einsum("sq,bsn->bqn", chosen, terms, precision=highest)
    mine = lax.psum_scatter(by_obs, "block", scatter_dimension=0, tiled=True)[0]
    everyone = lax.all_gather(mine, "dp", axis=0, tiled=True)
    jacobian = everyone[:, :block_order]
    predicted = everyone[:, -1]
    cov_rows = covariance[0]
    product = jnp.dot(cov_rows, jacobian.T, precision=highest)
    columns = lax.dynamic_slice_in_dim(jacobian, lax.axis_index("dp") * row_share, row_share, 1)
    partial_value = jnp.dot(columns, product, precision=highest)
    gram_sum = lax.psum(partial_value, ("dp", "block"))
    gram_sum = 0.5 * (gram_sum + gram_sum.T) + jnp.diag(noise_level)
    factor = jnp.linalg.cholesky(gram_sum)
    inverse = jax.scipy.linalg.cho_solve((factor, True), jnp.eye(OBS, dtype=jnp.float32))
    gain_rows = jnp.dot(product, inverse, precision=highest)
    product_all = lax.all_gather(product, "dp", axis=0, tiled=True)
    update = jnp.dot(gain_rows, product_all.T, precision=highest)
    innovation = targets - predicted
    block_window = lax.dynamic_slice_in_dim(
        window.reshape(block_count, block_order), lax.axis_index("block"), 1, 0
    )
    window_rows = lax.dynamic_slice_in_dim(
        block_window, lax.axis_index("dp") * row_share, row_share, 1
    )
    new_weights = window_rows + jnp.dot(gain_rows, innovation, precision=highest)[None, :]
    new_covariance = ((cov_rows - update) / forgetting)[None]
    return (new_weights, new_covariance)


def solution(mesh):
    return jax.shard_map(
        local,
        mesh=mesh,
        in_specs=(
            P(None, ("dp", "block")),
            P(None, ("dp", "block")),
            P(("dp", "block")),
            P(("dp", "block")),
            P(("dp", "block")),
            P(),
            P(),
            P(),
            P(),
            P(),
            P(),
            P(),
            P(),
            P(),
            P("block", "dp", None),
        ),
        out_specs=(P("block", "dp"), P("block", "dp", None)),
        check_vma=False,
    )
```

```python
import functools

import jax
import jax.numpy as jnp
from jax import lax
from jax.experimental import pallas as pl
from jax.experimental.pallas import tpu as pltpu
from jax.sharding import PartitionSpec as P

OBS = 64
AUX = 128

radial_width = 4.0
forgetting = 0.98
highest = lax.Precision.HIGHEST


def contract(left, right, left_dim, right_dim):
    return lax.dot_general(
        left,
        right,
        (((left_dim,), (right_dim,)), ((), ())),
        precision=highest,
        preferred_element_type=jnp.float32,
    )


def observe_kernel(
    weighting,
    tagged_ref,
    observed_ref,
    positions_ref,
    neighbours_ref,
    species_ref,
    scale_ref,
    shift_ref,
    first_weight_ref,
    first_bias_ref,
    middle_ref,
    middle_bias_ref,
    energy_ref,
    out_ref,
    radial_ref,
    slope_ref,
    near_ref,
    scale_cols,
    shift_cols,
    desc_ref,
):
    atoms = positions_ref.shape[1]
    structs = tagged_ref.shape[1]
    struct_size = atoms // structs
    slots = neighbours_ref.shape[0]
    species_count, channels = scale_ref.shape
    hidden = middle_ref.shape[1]
    blocks = out_ref.shape[0]
    order = out_ref.shape[2] - AUX
    block_rows = order // hidden
    rows = blocks * block_rows

    lane = lax.broadcasted_iota(jnp.int32, (1, atoms), 1)
    start = jnp.zeros_like(lane)
    tag = jnp.zeros_like(lane)
    comp = jnp.zeros_like(lane)
    for s in range(structs):
        here = jnp.logical_and(lane >= s * struct_size, lane < (s + 1) * struct_size)
        start = jnp.where(here, s * struct_size, start)
        tag = jnp.where(here, tagged_ref[0, s], tag)
        comp = jnp.where(here, observed_ref[0, s] & 3, comp)
    inside = lane - start
    own = species_ref[...]

    for base in range(0, atoms, 128):
        cols = slice(base, base + 128)
        listed = neighbours_ref[:, cols]
        near = jnp.minimum(listed, struct_size - 1)
        index = near + (start[:, cols] - base)

        def pick(row):
            wide = jnp.broadcast_to(row, (slots, 128))
            return jnp.take_along_axis(wide, index, axis=1, mode="promise_in_bounds")

        shift_by = []
        for axis in range(3):
            mine = positions_ref[axis : axis + 1, cols]
            shift_by.append(pick(mine) - mine)
        distance_sq = shift_by[0] * shift_by[0]
        for axis in range(1, 3):
            distance_sq = distance_sq + shift_by[axis] * shift_by[axis]
        live = listed < struct_size
        radial = jnp.where(live, jnp.exp(-distance_sq / radial_width), 0.0)
        near_species = pick(own[:, cols].astype(jnp.float32))
        kind = comp[:, cols]
        along = jnp.where(kind == 1, shift_by[0], 0.0)
        along = jnp.where(kind == 2, shift_by[1], along)
        along = jnp.where(kind == 3, shift_by[2], along)
        moved = (near == tag[:, cols]).astype(jnp.float32) - (
            inside[:, cols] == tag[:, cols]
        ).astype(jnp.float32)
        slope = (-2.0 / radial_width) * radial * along * moved
        for k in range(slots):
            radial_ref[k, :, cols] = jnp.broadcast_to(radial[k : k + 1], (8, 128))
            slope_ref[k, :, cols] = jnp.broadcast_to(slope[k : k + 1], (8, 128))
            near_ref[k, :, cols] = jnp.broadcast_to(near_species[k : k + 1], (8, 128))

    scale_t = scale_ref[...].T
    shift_t = shift_ref[...].T
    for i in range(species_count):
        scale_cols[i] = jnp.broadcast_to(scale_t[:, i : i + 1], (channels, 128))
        shift_cols[i] = jnp.broadcast_to(shift_t[:, i : i + 1], (channels, 128))

    def embed(group, _):
        group_rows = pl.ds(pl.multiple_of(group * 8, 8), 8)
        scales = [scale_cols[i, group_rows, :] for i in range(species_count)]
        shifts = [shift_cols[i, group_rows, :] for i in range(species_count)]
        for base in range(0, atoms, 128):
            cols = slice(base, base + 128)
            total = jnp.zeros((8, 128), jnp.float32)
            moved = jnp.zeros((8, 128), jnp.float32)
            for k in range(slots):
                radial = radial_ref[k, :, cols]
                slope = slope_ref[k, :, cols]
                near = near_ref[k, :, cols]
                scale, shift = scales[-1], shifts[-1]
                for i in range(species_count - 1):
                    same = near == float(i)
                    scale = jnp.where(same, scales[i], scale)
                    shift = jnp.where(same, shifts[i], shift)
                scaled = radial * scale
                bent = jnp.tanh(scaled + shift)
                total = total + radial * bent
                moved = moved + slope * (bent + scaled * (1.0 - bent * bent))
            desc_ref[group_rows, cols] = total * (1.0 / slots)
            desc_ref[group_rows, slice(atoms + base, atoms + base + 128)] = moved * (
                1.0 / slots
            )
        return 0

    lax.fori_loop(0, channels // 8, embed, 0)

    first_bias = jnp.broadcast_to(first_bias_ref[...], (8, hidden)).T[:, :1]
    middle_bias = jnp.broadcast_to(middle_bias_ref[...], (8, hidden)).T[:, :1]
    energy_t = energy_ref[...].T
    lower = contract(first_weight_ref[...], desc_ref[...], 0, 0)
    first = jnp.tanh(lower[:, :atoms] + first_bias)
    first_moved = (1.0 - first * first) * lower[:, atoms:]
    upper = contract(middle_ref[...], jnp.concatenate([first, first_moved], axis=1), 0, 0)
    second = jnp.tanh(upper[:, :atoms] + middle_bias)
    moved = upper[:, atoms:]
    readout = jnp.broadcast_to(
        energy_t[:, species_count - 1 : species_count], (hidden, atoms)
    )
    for i in range(species_count - 1):
        readout = jnp.where(own == i, energy_t[:, i : i + 1], readout)
    gate = readout * (1.0 - second * second)
    mean = jnp.where(comp == 0, 1.0 / struct_size, 0.0)
    value = mean * jnp.sum(readout * second, axis=0, keepdims=True) - jnp.sum(
        gate * moved, axis=0, keepdims=True
    )
    bend = 2.0 * second * gate * moved + mean * gate

    struct_row = lax.broadcasted_iota(jnp.int32, (structs, atoms), 0)
    member = jnp.where(start == struct_row * struct_size, weighting, 0.0)
    struct_value = jnp.sum(member * value, axis=1, keepdims=True)
    left = jnp.concatenate([-first_moved[:rows], first[:rows]], axis=1)
    right = jnp.concatenate([gate, bend], axis=1)
    member_twice = jnp.concatenate([member, member], axis=1)
    spread = (left[:, None, :] * member_twice[None]).reshape(rows * structs, 2 * atoms)
    terms = contract(spread, right, 1, 1)
    for h in range(rows):
        place = AUX + (h % block_rows) * hidden
        out_ref[h // block_rows, :, place : place + hidden] = terms[
            h * structs : (h + 1) * structs
        ]
    row = lax.broadcasted_iota(jnp.int32, (structs, AUX), 0)
    column = lax.broadcasted_iota(jnp.int32, (structs, AUX), 1)
    observed = jnp.zeros((structs, AUX), jnp.int32)
    for s in range(structs):
        observed = jnp.where(row == s, observed_ref[0, s], observed)
    aux = jnp.where(
        column < OBS, (observed == column).astype(jnp.float32), struct_value
    )
    for b in range(blocks):
        out_ref[b, :, :AUX] = aux


def observe(
    blocks,
    order,
    weighting,
    positions,
    neighbours,
    atom_species,
    tagged_atom,
    observed_in,
    embed_scale,
    embed_shift,
    first_weight,
    first_bias,
    middle_weight,
    middle_bias,
    energy_weight,
):
    atoms = positions.shape[1]
    structs = tagged_atom.shape[0]
    slots = neighbours.shape[0]
    species_count, channels = embed_scale.shape
    vmem = pl.BlockSpec(memory_space=pltpu.VMEM)
    smem = pl.BlockSpec(memory_space=pltpu.SMEM)
    return pl.pallas_call(
        functools.partial(observe_kernel, weighting),
        out_shape=jax.ShapeDtypeStruct((blocks, structs, order + AUX), jnp.float32),
        in_specs=[smem, smem] + [vmem] * 10,
        out_specs=vmem,
        scratch_shapes=[
            pltpu.VMEM((slots, 8, atoms), jnp.float32),
            pltpu.VMEM((slots, 8, atoms), jnp.float32),
            pltpu.VMEM((slots, 8, atoms), jnp.float32),
            pltpu.VMEM((species_count, channels, 128), jnp.float32),
            pltpu.VMEM((species_count, channels, 128), jnp.float32),
            pltpu.VMEM((channels, 2 * atoms), jnp.float32),
        ],
    )(
        tagged_atom[None],
        observed_in[None],
        positions,
        neighbours,
        atom_species[None],
        embed_scale,
        embed_shift,
        first_weight,
        first_bias[None],
        middle_weight,
        middle_bias[None],
        energy_weight,
    )


MESH = pl.DeviceIdType.MESH


def exchange_kernel(
    group_count,
    block_count,
    terms_ref,
    cov_ref,
    product_ref,
    gram_ref,
    aux_ref,
    got,
    jac,
    cov_rows,
    total,
    gram_mine,
    gram_near,
    gram_sum,
    gram_far,
    cov_sem,
    own_sem,
    term_send,
    term_recv,
    jac_send,
    jac_recv,
    gram_send,
    gram_recv,
    far_send,
    far_recv,
    product_send,
    product_recv,
):
    group = lax.axis_index("dp")
    block = lax.axis_index("block")
    structs, width = terms_ref.shape[1:]
    obs_group = jac.shape[1]
    row_share = cov_ref.shape[0]
    half = (width - AUX) // 2
    chunks = ((0, AUX + half), (AUX + half, half))
    group_peers = [(o, lax.rem(group + o, group_count)) for o in range(1, group_count)]
    block_peers = [(o, lax.rem(block + o, block_count)) for o in range(1, block_count)]

    cov_copy = pltpu.make_async_copy(cov_ref, cov_rows, cov_sem)
    cov_copy.start()
    own_copy = pltpu.make_async_copy(terms_ref.at[block], got.at[0], own_sem)
    own_copy.start()

    barrier = pltpu.get_barrier_semaphore()
    for _, peer in group_peers:
        pl.semaphore_signal(
            barrier, inc=1, device_id={"dp": peer}, device_id_type=MESH
        )
    for _, peer in block_peers:
        pl.semaphore_signal(
            barrier, inc=1, device_id={"block": peer}, device_id_type=MESH
        )
    pl.semaphore_wait(barrier, group_count + block_count - 2)

    def send(source, target, send_sem, recv_sem, device_id):
        copy = pltpu.make_async_remote_copy(
            src_ref=source,
            dst_ref=target,
            send_sem=send_sem,
            recv_sem=recv_sem,
            device_id=device_id,
            device_id_type=MESH,
        )
        copy.start()
        return copy

    term_copies = []
    for c, (base, size) in enumerate(chunks):
        cols = pl.ds(base, size)
        term_copies.append(
            [
                send(
                    terms_ref.at[peer, :, cols],
                    got.at[o, :, cols],
                    term_send.at[c, o - 1],
                    term_recv.at[c, o - 1],
                    {"block": peer},
                )
                for o, peer in block_peers
            ]
        )
    own_copy.wait()

    jac_copies = []
    for c, (base, size) in enumerate(chunks):
        cols = pl.ds(base, size)
        for copy in term_copies[c]:
            copy.wait_recv()
        chosen = got[:, :, :AUX].reshape(block_count * structs, AUX).T[:obs_group]
        pieces = got[:, :, cols].reshape(block_count * structs, size)
        jac[group, :, cols] = contract(chosen, pieces, 1, 0)
        jac_copies.append(
            [
                send(
                    jac.at[group, :, cols],
                    jac.at[group, :, cols],
                    jac_send.at[c, o - 1],
                    jac_recv.at[c, o - 1],
                    {"dp": peer},
                )
                for o, peer in group_peers
            ]
        )

    cov_copy.wait()
    for c in range(2):
        for copy in jac_copies[c]:
            copy.wait_recv()
        rows = jac[:, :, AUX + c * half : AUX + (c + 1) * half].reshape(OBS, half)
        rows = jnp.concatenate([rows, jnp.zeros_like(rows)], axis=0)
        part = contract(cov_rows[:, c * half : (c + 1) * half], rows, 1, 1)
        if c == 0:
            total[...] = part
        else:
            product = (total[...] + part).T
    product_ref[group] = product[:OBS]
    mine = jac[:, :, pl.ds(pl.multiple_of(AUX + group * row_share, 128), row_share)]
    gram = contract(mine.reshape(OBS, row_share), product, 1, 1)
    fold = OBS // 2
    gram_mine[...] = gram[:fold] + pltpu.roll(gram[fold:], 64, 1)
    gram_copies = [
        send(
            gram_mine,
            gram_near.at[o - 1],
            gram_send.at[o - 1],
            gram_recv.at[o - 1],
            {"dp": peer},
        )
        for o, peer in group_peers
    ]
    product_copies = [
        send(
            product_ref.at[group],
            product_ref.at[group],
            product_send.at[o - 1],
            product_recv.at[o - 1],
            {"dp": peer},
        )
        for o, peer in group_peers
    ]
    aux_ref[...] = jac[:, :, :AUX]
    summed = gram_mine[...]
    for i, copy in enumerate(gram_copies):
        copy.wait_recv()
        summed = summed + gram_near[i]
    gram_sum[...] = summed
    far_copies = [
        send(
            gram_sum,
            gram_far.at[o - 1],
            far_send.at[o - 1],
            far_recv.at[o - 1],
            {"block": peer},
        )
        for o, peer in block_peers
    ]
    for i, copy in enumerate(far_copies):
        copy.wait_recv()
        summed = summed + gram_far[i]
    gram_ref[:fold] = summed
    gram_ref[fold:] = pltpu.roll(summed, 64, 1)
    for copy in product_copies:
        copy.wait_recv()
    for copies in term_copies + jac_copies + [gram_copies, far_copies, product_copies]:
        for copy in copies:
            copy.wait_send()


def exchange(group_count, obs_group, terms, cov_rows):
    block_count, structs, width = terms.shape
    row_share, order = cov_rows.shape
    vmem = pl.BlockSpec(memory_space=pltpu.VMEM)
    fold = OBS // 2
    dma = pltpu.SemaphoreType.DMA
    near, far = group_count - 1, block_count - 1
    return pl.pallas_call(
        functools.partial(exchange_kernel, group_count, block_count),
        out_shape=(
            jax.ShapeDtypeStruct((group_count, OBS, row_share), jnp.float32),
            jax.ShapeDtypeStruct((OBS, 128), jnp.float32),
            jax.ShapeDtypeStruct((group_count, obs_group, AUX), jnp.float32),
        ),
        in_specs=[vmem, pl.BlockSpec(memory_space=pl.ANY)],
        out_specs=(vmem, vmem, vmem),
        scratch_shapes=[
            pltpu.VMEM((block_count, structs, width), jnp.float32),
            pltpu.VMEM((group_count, obs_group, width), jnp.float32),
            pltpu.VMEM((row_share, order), jnp.float32),
            pltpu.VMEM((row_share, 128), jnp.float32),
            pltpu.VMEM((fold, 128), jnp.float32),
            pltpu.VMEM((near, fold, 128), jnp.float32),
            pltpu.VMEM((fold, 128), jnp.float32),
            pltpu.VMEM((far, fold, 128), jnp.float32),
            dma,
            dma,
            dma((2, far)),
            dma((2, far)),
            dma((2, near)),
            dma((2, near)),
            dma((near,)),
            dma((near,)),
            dma((far,)),
            dma((far,)),
            dma((near,)),
            dma((near,)),
        ],
        compiler_params=pltpu.CompilerParams(collective_id=0, has_side_effects=True),
    )(terms, cov_rows)


def update_kernel(
    gram_ref,
    product_ref,
    aux_ref,
    targets_ref,
    noise_ref,
    middle_ref,
    cov_ref,
    weights_ref,
    new_cov_ref,
    gain_ref,
):
    step = pl.program_id(0)
    tile, order = cov_ref.shape
    row_share = product_ref.shape[2]
    hidden = middle_ref.shape[1]

    @pl.when(step == 0)
    def _():
        row = lax.broadcasted_iota(jnp.int32, (OBS, OBS), 0)
        column = lax.broadcasted_iota(jnp.int32, (OBS, OBS), 1)
        gram = gram_ref[...]
        pad = jnp.zeros((128 - OBS, 128), jnp.float32)
        flipped = jnp.concatenate([gram, pad], axis=0).T[:OBS]
        matrix = 0.5 * (gram + flipped)[:, :OBS]
        matrix = matrix + jnp.where(row == column, noise_ref[...], 0.0)
        for k in range(OBS):
            pivot = 1.0 / matrix[k : k + 1, k : k + 1]
            scaled = jnp.where(column[:1] == k, pivot, matrix[k : k + 1] * pivot)
            side = jnp.where(row[:, :1] == k, -1.0, matrix[:, k : k + 1])
            kept = jnp.where(jnp.logical_or(row == k, column == k), 0.0, matrix)
            matrix = kept - side * scaled
        group = lax.axis_index("dp")
        gain = contract(product_ref[group], matrix, 0, 0)
        gain_ref[...] = gain
        predicted = jnp.sum(
            jnp.where(row == column, aux_ref[:, 128 - OBS :], 0.0), axis=0, keepdims=True
        )
        innovation = jnp.broadcast_to(targets_ref[...] - predicted, (8, OBS))
        moved = contract(innovation, gain, 1, 1)[:1]
        first = lax.axis_index("block") * order + group * row_share
        for i in range(row_share // 128):
            flat = first + i * 128
            line = middle_ref[pl.ds(flat // hidden, 1), :]
            window = line[:, :128]
            for j in range(1, hidden // 128):
                window = jnp.where(
                    lax.rem(flat, hidden) == j * 128,
                    line[:, j * 128 : (j + 1) * 128],
                    window,
                )
            here = slice(i * 128, (i + 1) * 128)
            weights_ref[:, here] = window + moved[:, here]

    gain = gain_ref[pl.ds(pl.multiple_of(step * tile, tile), tile), :]
    for d in range(product_ref.shape[0]):
        cols = slice(d * row_share, (d + 1) * row_share)
        update = contract(gain, product_ref[d], 1, 0)
        new_cov_ref[:, cols] = (cov_ref[:, cols] - update) * (1.0 / forgetting)


def update(gram, product, aux, targets, noise_level, middle_weight, cov_rows):
    row_share, order = cov_rows.shape
    tile = min(128, row_share)
    vmem = pl.BlockSpec(memory_space=pltpu.VMEM)
    cov_spec = pl.BlockSpec((tile, order), lambda i: (i, 0))
    return pl.pallas_call(
        update_kernel,
        grid=(row_share // tile,),
        out_shape=(
            jax.ShapeDtypeStruct((1, row_share), jnp.float32),
            jax.ShapeDtypeStruct((row_share, order), jnp.float32),
        ),
        in_specs=[vmem] * 6 + [cov_spec],
        out_specs=(pl.BlockSpec((1, row_share), lambda i: (0, 0)), cov_spec),
        scratch_shapes=[pltpu.VMEM((row_share, OBS), jnp.float32)],
    )(
        gram,
        product,
        aux.reshape(OBS, AUX),
        targets[None],
        noise_level[None],
        middle_weight,
        cov_rows,
    )


def local(
    positions,
    neighbours,
    atom_species,
    tagged_atom,
    observed_in,
    targets,
    noise_level,
    embed_scale,
    embed_shift,
    first_weight,
    first_bias,
    middle_weight,
    middle_bias,
    energy_weight,
    covariance,
):
    group_count = lax.axis_size("dp")
    block_count = lax.axis_size("block")
    block_order = covariance.shape[2]
    obs_group = OBS // group_count
    weighting = OBS / (tagged_atom.shape[0] * group_count * block_count)
    terms = observe(
        block_count,
        block_order,
        weighting,
        positions,
        neighbours,
        atom_species,
        tagged_atom,
        observed_in,
        embed_scale,
        embed_shift,
        first_weight,
        first_bias,
        middle_weight,
        middle_bias,
        energy_weight,
    )
    product, gram, aux = exchange(group_count, obs_group, terms, covariance[0])
    new_weights, new_rows = update(
        gram, product, aux, targets, noise_level, middle_weight, covariance[0]
    )
    return (new_weights, new_rows[None])


def solution(mesh):
    return jax.shard_map(
        local,
        mesh=mesh,
        in_specs=(
            P(None, ("dp", "block")),
            P(None, ("dp", "block")),
            P(("dp", "block")),
            P(("dp", "block")),
            P(("dp", "block")),
            P(),
            P(),
            P(),
            P(),
            P(),
            P(),
            P(),
            P(),
            P(),
            P("block", "dp", None),
        ),
        out_specs=(P("block", "dp"), P("block", "dp", None)),
        check_vma=False,
    )
```

```python
import functools

import jax
import jax.numpy as jnp
from jax import lax
from jax.experimental import pallas as pl
from jax.experimental.pallas import tpu as pltpu
from jax.sharding import PartitionSpec as P

OBS = 64
AUX = 128
CHUNKS = 4

radial_width = 4.0
forgetting = 0.98


def halves(value):
    high = value.astype(jnp.bfloat16)
    return high, (value - high.astype(jnp.float32)).astype(jnp.bfloat16)


def contract(left, right, left_dim, right_dim, exact_left=False):
    def one(a, b):
        return lax.dot_general(
            a,
            b,
            (((left_dim,), (right_dim,)), ((), ())),
            preferred_element_type=jnp.float32,
        )

    right_high, right_low = halves(right)
    left_high, left_low = halves(left)
    small = one(left_high, right_low)
    if not exact_left:
        small = small + one(left_low, right_high)
    return small + one(left_high, right_high)


def observe_kernel(
    weighting,
    tagged_ref,
    observed_ref,
    positions_ref,
    neighbours_ref,
    species_ref,
    scale_ref,
    shift_ref,
    first_weight_ref,
    first_bias_ref,
    middle_ref,
    middle_bias_ref,
    energy_ref,
    out_ref,
    radial_ref,
    slope_ref,
    near_ref,
    scale_cols,
    shift_cols,
    desc_ref,
):
    atoms = positions_ref.shape[1]
    structs = tagged_ref.shape[1]
    struct_size = atoms // structs
    slots = neighbours_ref.shape[0]
    species_count, channels = scale_ref.shape
    hidden = middle_ref.shape[1]
    blocks = out_ref.shape[0]
    order = out_ref.shape[2] - AUX
    block_rows = order // hidden
    rows = blocks * block_rows

    lane = lax.broadcasted_iota(jnp.int32, (1, atoms), 1)
    start = jnp.zeros_like(lane)
    tag = jnp.zeros_like(lane)
    comp = jnp.zeros_like(lane)
    for s in range(structs):
        here = jnp.logical_and(lane >= s * struct_size, lane < (s + 1) * struct_size)
        start = jnp.where(here, s * struct_size, start)
        tag = jnp.where(here, tagged_ref[0, s], tag)
        comp = jnp.where(here, observed_ref[0, s] & 3, comp)
    inside = lane - start
    own = species_ref[...]

    for base in range(0, atoms, 128):
        cols = slice(base, base + 128)
        listed = neighbours_ref[:, cols]
        near = jnp.minimum(listed, struct_size - 1)
        index = near + (start[:, cols] - base)

        def pick(row):
            wide = jnp.broadcast_to(row, (slots, 128))
            return jnp.take_along_axis(wide, index, axis=1, mode="promise_in_bounds")

        shift_by = []
        for axis in range(3):
            mine = positions_ref[axis : axis + 1, cols]
            shift_by.append(pick(mine) - mine)
        distance_sq = shift_by[0] * shift_by[0]
        for axis in range(1, 3):
            distance_sq = distance_sq + shift_by[axis] * shift_by[axis]
        live = listed < struct_size
        radial = jnp.where(live, jnp.exp(-distance_sq / radial_width), 0.0)
        near_species = pick(own[:, cols].astype(jnp.float32))
        kind = comp[:, cols]
        along = jnp.where(kind == 1, shift_by[0], 0.0)
        along = jnp.where(kind == 2, shift_by[1], along)
        along = jnp.where(kind == 3, shift_by[2], along)
        moved = (near == tag[:, cols]).astype(jnp.float32) - (
            inside[:, cols] == tag[:, cols]
        ).astype(jnp.float32)
        slope = (-2.0 / radial_width) * radial * along * moved
        for k in range(slots):
            radial_ref[k, :, cols] = jnp.broadcast_to(radial[k : k + 1], (8, 128))
            slope_ref[k, :, cols] = jnp.broadcast_to(slope[k : k + 1], (8, 128))
            near_ref[k, :, cols] = jnp.broadcast_to(near_species[k : k + 1], (8, 128))

    scale_t = scale_ref[...].T
    shift_t = shift_ref[...].T
    for i in range(species_count):
        scale_cols[i] = jnp.broadcast_to(scale_t[:, i : i + 1], (channels, 128))
        shift_cols[i] = jnp.broadcast_to(shift_t[:, i : i + 1], (channels, 128))

    def embed(group, _):
        group_rows = pl.ds(pl.multiple_of(group * 8, 8), 8)
        scales = [scale_cols[i, group_rows, :] for i in range(species_count)]
        shifts = [shift_cols[i, group_rows, :] for i in range(species_count)]
        for base in range(0, atoms, 128):
            cols = slice(base, base + 128)
            total = jnp.zeros((8, 128), jnp.float32)
            moved = jnp.zeros((8, 128), jnp.float32)
            for k in range(slots):
                radial = radial_ref[k, :, cols]
                slope = slope_ref[k, :, cols]
                near = near_ref[k, :, cols]
                scale, shift = scales[-1], shifts[-1]
                for i in range(species_count - 1):
                    same = near == float(i)
                    scale = jnp.where(same, scales[i], scale)
                    shift = jnp.where(same, shifts[i], shift)
                scaled = radial * scale
                bent = jnp.tanh(scaled + shift)
                total = total + radial * bent
                moved = moved + slope * (bent + scaled * (1.0 - bent * bent))
            desc_ref[group_rows, cols] = total * (1.0 / slots)
            desc_ref[group_rows, slice(atoms + base, atoms + base + 128)] = moved * (
                1.0 / slots
            )
        return 0

    lax.fori_loop(0, channels // 8, embed, 0)

    first_bias = jnp.broadcast_to(first_bias_ref[...], (8, hidden)).T[:, :1]
    middle_bias = jnp.broadcast_to(middle_bias_ref[...], (8, hidden)).T[:, :1]
    energy_t = energy_ref[...].T
    lower = contract(first_weight_ref[...], desc_ref[...], 0, 0)
    first = jnp.tanh(lower[:, :atoms] + first_bias)
    first_moved = (1.0 - first * first) * lower[:, atoms:]
    upper = contract(middle_ref[...], jnp.concatenate([first, first_moved], axis=1), 0, 0)
    second = jnp.tanh(upper[:, :atoms] + middle_bias)
    moved = upper[:, atoms:]
    readout = jnp.broadcast_to(
        energy_t[:, species_count - 1 : species_count], (hidden, atoms)
    )
    for i in range(species_count - 1):
        readout = jnp.where(own == i, energy_t[:, i : i + 1], readout)
    gate = readout * (1.0 - second * second)
    mean = jnp.where(comp == 0, 1.0 / struct_size, 0.0)
    value = mean * jnp.sum(readout * second, axis=0, keepdims=True) - jnp.sum(
        gate * moved, axis=0, keepdims=True
    )
    bend = 2.0 * second * gate * moved + mean * gate

    struct_row = lax.broadcasted_iota(jnp.int32, (structs, atoms), 0)
    member = jnp.where(start == struct_row * struct_size, weighting, 0.0)
    struct_value = jnp.sum(member * value, axis=1, keepdims=True)
    left = jnp.concatenate([-first_moved[:rows], first[:rows]], axis=1)
    right = jnp.concatenate([gate, bend], axis=1)
    member_twice = jnp.concatenate([member, member], axis=1)
    spread = (left[:, None, :] * member_twice[None]).reshape(rows * structs, 2 * atoms)
    terms = contract(spread, right, 1, 1)
    for h in range(rows):
        place = AUX + (h % block_rows) * hidden
        out_ref[h // block_rows, :, place : place + hidden] = terms[
            h * structs : (h + 1) * structs
        ]
    row = lax.broadcasted_iota(jnp.int32, (structs, AUX), 0)
    column = lax.broadcasted_iota(jnp.int32, (structs, AUX), 1)
    observed = jnp.zeros((structs, AUX), jnp.int32)
    for s in range(structs):
        observed = jnp.where(row == s, observed_ref[0, s], observed)
    aux = jnp.where(
        column < OBS, (observed == column).astype(jnp.float32), struct_value
    )
    for b in range(blocks):
        out_ref[b, :, :AUX] = aux


def observe(
    blocks,
    order,
    weighting,
    positions,
    neighbours,
    atom_species,
    tagged_atom,
    observed_in,
    embed_scale,
    embed_shift,
    first_weight,
    first_bias,
    middle_weight,
    middle_bias,
    energy_weight,
):
    atoms = positions.shape[1]
    structs = tagged_atom.shape[0]
    slots = neighbours.shape[0]
    species_count, channels = embed_scale.shape
    vmem = pl.BlockSpec(memory_space=pltpu.VMEM)
    smem = pl.BlockSpec(memory_space=pltpu.SMEM)
    return pl.pallas_call(
        functools.partial(observe_kernel, weighting),
        out_shape=jax.ShapeDtypeStruct((blocks, structs, order + AUX), jnp.float32),
        in_specs=[smem, smem] + [vmem] * 10,
        out_specs=vmem,
        scratch_shapes=[
            pltpu.VMEM((slots, 8, atoms), jnp.float32),
            pltpu.VMEM((slots, 8, atoms), jnp.float32),
            pltpu.VMEM((slots, 8, atoms), jnp.float32),
            pltpu.VMEM((species_count, channels, 128), jnp.float32),
            pltpu.VMEM((species_count, channels, 128), jnp.float32),
            pltpu.VMEM((channels, 2 * atoms), jnp.float32),
        ],
    )(
        tagged_atom[None],
        observed_in[None],
        positions,
        neighbours,
        atom_species[None],
        embed_scale,
        embed_shift,
        first_weight,
        first_bias[None],
        middle_weight,
        middle_bias[None],
        energy_weight,
    )


MESH = pl.DeviceIdType.MESH


def exchange_kernel(
    group_count,
    block_count,
    terms_ref,
    cov_ref,
    product_ref,
    gram_ref,
    aux_ref,
    got,
    jac,
    cov_rows,
    total,
    gram_mine,
    gram_near,
    gram_sum,
    gram_far,
    cov_sem,
    own_sem,
    term_send,
    term_recv,
    jac_send,
    jac_recv,
    gram_send,
    gram_recv,
    far_send,
    far_recv,
    product_send,
    product_recv,
):
    group = lax.axis_index("dp")
    block = lax.axis_index("block")
    structs, width = terms_ref.shape[1:]
    obs_group = jac.shape[1]
    row_share = cov_ref.shape[0]
    piece = (width - AUX) // CHUNKS
    chunks = [(0, AUX + piece)]
    chunks += [(AUX + c * piece, piece) for c in range(1, CHUNKS)]
    group_peers = [(o, lax.rem(group + o, group_count)) for o in range(1, group_count)]
    block_peers = [(o, lax.rem(block + o, block_count)) for o in range(1, block_count)]

    cov_copy = pltpu.make_async_copy(cov_ref, cov_rows, cov_sem)
    cov_copy.start()
    own_copy = pltpu.make_async_copy(terms_ref.at[block], got.at[0], own_sem)
    own_copy.start()

    barrier = pltpu.get_barrier_semaphore()
    for _, peer in group_peers:
        pl.semaphore_signal(
            barrier, inc=1, device_id={"dp": peer}, device_id_type=MESH
        )
    for _, peer in block_peers:
        pl.semaphore_signal(
            barrier, inc=1, device_id={"block": peer}, device_id_type=MESH
        )
    pl.semaphore_wait(barrier, group_count + block_count - 2)

    def send(source, target, send_sem, recv_sem, device_id):
        copy = pltpu.make_async_remote_copy(
            src_ref=source,
            dst_ref=target,
            send_sem=send_sem,
            recv_sem=recv_sem,
            device_id=device_id,
            device_id_type=MESH,
        )
        copy.start()
        return copy

    term_copies = []
    for c, (base, size) in enumerate(chunks):
        cols = pl.ds(base, size)
        term_copies.append(
            [
                send(
                    terms_ref.at[peer, :, cols],
                    got.at[o, :, cols],
                    term_send.at[c, o - 1],
                    term_recv.at[c, o - 1],
                    {"block": peer},
                )
                for o, peer in block_peers
            ]
        )
    own_copy.wait()

    jac_copies = []
    for c, (base, size) in enumerate(chunks):
        cols = pl.ds(base, size)
        for copy in term_copies[c]:
            copy.wait_recv()
        chosen = got[:, :, :AUX].reshape(block_count * structs, AUX).T[:obs_group]
        pieces = got[:, :, cols].reshape(block_count * structs, size)
        jac[group, :, cols] = contract(chosen, pieces, 1, 0, exact_left=True)
        jac_copies.append(
            [
                send(
                    jac.at[group, :, cols],
                    jac.at[group, :, cols],
                    jac_send.at[c, o - 1],
                    jac_recv.at[c, o - 1],
                    {"dp": peer},
                )
                for o, peer in group_peers
            ]
        )

    cov_copy.wait()
    for c in range(CHUNKS):
        for copy in jac_copies[c]:
            copy.wait_recv()
        rows = jac[:, :, AUX + c * piece : AUX + (c + 1) * piece].reshape(OBS, piece)
        rows = jnp.concatenate([rows, jnp.zeros_like(rows)], axis=0)
        part = contract(cov_rows[:, c * piece : (c + 1) * piece], rows, 1, 1)
        total[...] = part if c == 0 else total[...] + part
    product = total[...].T
    product_ref[group] = product[:OBS]
    mine = jac[:, :, pl.ds(pl.multiple_of(AUX + group * row_share, 128), row_share)]
    gram = contract(mine.reshape(OBS, row_share), product, 1, 1)
    fold = OBS // 2
    gram_mine[...] = gram[:fold] + pltpu.roll(gram[fold:], 64, 1)
    gram_copies = [
        send(
            gram_mine,
            gram_near.at[o - 1],
            gram_send.at[o - 1],
            gram_recv.at[o - 1],
            {"dp": peer},
        )
        for o, peer in group_peers
    ]
    product_copies = [
        send(
            product_ref.at[group],
            product_ref.at[group],
            product_send.at[o - 1],
            product_recv.at[o - 1],
            {"dp": peer},
        )
        for o, peer in group_peers
    ]
    aux_ref[...] = jac[:, :, :AUX]
    summed = gram_mine[...]
    for i, copy in enumerate(gram_copies):
        copy.wait_recv()
        summed = summed + gram_near[i]
    gram_sum[...] = summed
    far_copies = [
        send(
            gram_sum,
            gram_far.at[o - 1],
            far_send.at[o - 1],
            far_recv.at[o - 1],
            {"block": peer},
        )
        for o, peer in block_peers
    ]
    for i, copy in enumerate(far_copies):
        copy.wait_recv()
        summed = summed + gram_far[i]
    gram_ref[:fold] = summed
    gram_ref[fold:] = pltpu.roll(summed, 64, 1)
    for copy in product_copies:
        copy.wait_recv()
    for copies in term_copies + jac_copies + [gram_copies, far_copies, product_copies]:
        for copy in copies:
            copy.wait_send()


def exchange(group_count, obs_group, terms, cov_rows):
    block_count, structs, width = terms.shape
    row_share, order = cov_rows.shape
    vmem = pl.BlockSpec(memory_space=pltpu.VMEM)
    fold = OBS // 2
    dma = pltpu.SemaphoreType.DMA
    near, far = group_count - 1, block_count - 1
    return pl.pallas_call(
        functools.partial(exchange_kernel, group_count, block_count),
        out_shape=(
            jax.ShapeDtypeStruct((group_count, OBS, row_share), jnp.float32),
            jax.ShapeDtypeStruct((OBS, 128), jnp.float32),
            jax.ShapeDtypeStruct((group_count, obs_group, AUX), jnp.float32),
        ),
        in_specs=[vmem, pl.BlockSpec(memory_space=pl.ANY)],
        out_specs=(vmem, vmem, vmem),
        scratch_shapes=[
            pltpu.VMEM((block_count, structs, width), jnp.float32),
            pltpu.VMEM((group_count, obs_group, width), jnp.float32),
            pltpu.VMEM((row_share, order), jnp.float32),
            pltpu.VMEM((row_share, 128), jnp.float32),
            pltpu.VMEM((fold, 128), jnp.float32),
            pltpu.VMEM((near, fold, 128), jnp.float32),
            pltpu.VMEM((fold, 128), jnp.float32),
            pltpu.VMEM((far, fold, 128), jnp.float32),
            dma,
            dma,
            dma((CHUNKS, far)),
            dma((CHUNKS, far)),
            dma((CHUNKS, near)),
            dma((CHUNKS, near)),
            dma((near,)),
            dma((near,)),
            dma((far,)),
            dma((far,)),
            dma((near,)),
            dma((near,)),
        ],
        compiler_params=pltpu.CompilerParams(collective_id=0, has_side_effects=True),
    )(terms, cov_rows)


def update_kernel(
    gram_ref,
    product_ref,
    aux_ref,
    targets_ref,
    noise_ref,
    middle_ref,
    cov_ref,
    weights_ref,
    new_cov_ref,
    gain_ref,
):
    step = pl.program_id(0)
    tile, order = cov_ref.shape
    row_share = product_ref.shape[2]
    hidden = middle_ref.shape[1]

    @pl.when(step == 0)
    def _():
        row = lax.broadcasted_iota(jnp.int32, (OBS, OBS), 0)
        column = lax.broadcasted_iota(jnp.int32, (OBS, OBS), 1)
        gram = gram_ref[...]
        pad = jnp.zeros((128 - OBS, 128), jnp.float32)
        flipped = jnp.concatenate([gram, pad], axis=0).T[:OBS]
        matrix = 0.5 * (gram + flipped)[:, :OBS]
        matrix = matrix + jnp.where(row == column, noise_ref[...], 0.0)
        for k in range(OBS):
            pivot = 1.0 / matrix[k : k + 1, k : k + 1]
            scaled = jnp.where(column[:1] == k, pivot, matrix[k : k + 1] * pivot)
            side = jnp.where(row[:, :1] == k, -1.0, matrix[:, k : k + 1])
            kept = jnp.where(jnp.logical_or(row == k, column == k), 0.0, matrix)
            matrix = kept - side * scaled
        group = lax.axis_index("dp")
        gain = contract(product_ref[group], matrix, 0, 0)
        gain_ref[...] = gain
        predicted = jnp.sum(
            jnp.where(row == column, aux_ref[:, 128 - OBS :], 0.0), axis=0, keepdims=True
        )
        innovation = jnp.broadcast_to(targets_ref[...] - predicted, (8, OBS))
        moved = contract(innovation, gain, 1, 1)[:1]
        first = lax.axis_index("block") * order + group * row_share
        for i in range(row_share // 128):
            flat = first + i * 128
            line = middle_ref[pl.ds(flat // hidden, 1), :]
            window = line[:, :128]
            for j in range(1, hidden // 128):
                window = jnp.where(
                    lax.rem(flat, hidden) == j * 128,
                    line[:, j * 128 : (j + 1) * 128],
                    window,
                )
            here = slice(i * 128, (i + 1) * 128)
            weights_ref[:, here] = window + moved[:, here]

    gain = gain_ref[pl.ds(pl.multiple_of(step * tile, tile), tile), :]
    for d in range(product_ref.shape[0]):
        cols = slice(d * row_share, (d + 1) * row_share)
        update = contract(gain, product_ref[d], 1, 0)
        new_cov_ref[:, cols] = (cov_ref[:, cols] - update) * (1.0 / forgetting)


def update(gram, product, aux, targets, noise_level, middle_weight, cov_rows):
    row_share, order = cov_rows.shape
    tile = min(128, row_share)
    vmem = pl.BlockSpec(memory_space=pltpu.VMEM)
    cov_spec = pl.BlockSpec((tile, order), lambda i: (i, 0))
    return pl.pallas_call(
        update_kernel,
        grid=(row_share // tile,),
        out_shape=(
            jax.ShapeDtypeStruct((1, row_share), jnp.float32),
            jax.ShapeDtypeStruct((row_share, order), jnp.float32),
        ),
        in_specs=[vmem] * 6 + [cov_spec],
        out_specs=(pl.BlockSpec((1, row_share), lambda i: (0, 0)), cov_spec),
        scratch_shapes=[pltpu.VMEM((row_share, OBS), jnp.float32)],
    )(
        gram,
        product,
        aux.reshape(OBS, AUX),
        targets[None],
        noise_level[None],
        middle_weight,
        cov_rows,
    )


def local(
    positions,
    neighbours,
    atom_species,
    tagged_atom,
    observed_in,
    targets,
    noise_level,
    embed_scale,
    embed_shift,
    first_weight,
    first_bias,
    middle_weight,
    middle_bias,
    energy_weight,
    covariance,
):
    group_count = lax.axis_size("dp")
    block_count = lax.axis_size("block")
    block_order = covariance.shape[2]
    obs_group = OBS // group_count
    weighting = OBS / (tagged_atom.shape[0] * group_count * block_count)
    terms = observe(
        block_count,
        block_order,
        weighting,
        positions,
        neighbours,
        atom_species,
        tagged_atom,
        observed_in,
        embed_scale,
        embed_shift,
        first_weight,
        first_bias,
        middle_weight,
        middle_bias,
        energy_weight,
    )
    product, gram, aux = exchange(group_count, obs_group, terms, covariance[0])
    new_weights, new_rows = update(
        gram, product, aux, targets, noise_level, middle_weight, covariance[0]
    )
    return (new_weights, new_rows[None])


def solution(mesh):
    return jax.shard_map(
        local,
        mesh=mesh,
        in_specs=(
            P(None, ("dp", "block")),
            P(None, ("dp", "block")),
            P(("dp", "block")),
            P(("dp", "block")),
            P(("dp", "block")),
            P(),
            P(),
            P(),
            P(),
            P(),
            P(),
            P(),
            P(),
            P(),
            P("block", "dp", None),
        ),
        out_specs=(P("block", "dp"), P("block", "dp", None)),
        check_vma=False,
    )
```

```python
import functools

import jax
import jax.numpy as jnp
from jax import lax
from jax.experimental import pallas as pl
from jax.experimental.pallas import tpu as pltpu
from jax.sharding import PartitionSpec as P

OBS = 64
AUX = 128
CHUNKS = 4

radial_width = 4.0
forgetting = 0.98


def halves(value):
    high = value.astype(jnp.bfloat16)
    return high, (value - high.astype(jnp.float32)).astype(jnp.bfloat16)


def contract(left, right, left_dim, right_dim, exact_left=False):
    def one(a, b):
        return lax.dot_general(
            a,
            b,
            (((left_dim,), (right_dim,)), ((), ())),
            preferred_element_type=jnp.float32,
        )

    right_high, right_low = halves(right)
    left_high, left_low = halves(left)
    small = one(left_high, right_low)
    if not exact_left:
        small = small + one(left_low, right_high)
    return small + one(left_high, right_high)


def observe_kernel(
    weighting,
    tagged_ref,
    observed_ref,
    positions_ref,
    neighbours_ref,
    species_ref,
    scale_ref,
    shift_ref,
    first_weight_ref,
    first_bias_ref,
    middle_ref,
    middle_bias_ref,
    energy_ref,
    out_ref,
    radial_ref,
    slope_ref,
    near_ref,
    scale_cols,
    shift_cols,
    desc_ref,
):
    atoms = positions_ref.shape[1]
    structs = tagged_ref.shape[1]
    struct_size = atoms // structs
    slots = neighbours_ref.shape[0]
    species_count, channels = scale_ref.shape
    hidden = middle_ref.shape[1]
    blocks = out_ref.shape[0]
    order = out_ref.shape[2] - AUX
    block_rows = order // hidden
    rows = blocks * block_rows

    lane = lax.broadcasted_iota(jnp.int32, (1, atoms), 1)
    start = jnp.zeros_like(lane)
    tag = jnp.zeros_like(lane)
    comp = jnp.zeros_like(lane)
    for s in range(structs):
        here = jnp.logical_and(lane >= s * struct_size, lane < (s + 1) * struct_size)
        start = jnp.where(here, s * struct_size, start)
        tag = jnp.where(here, tagged_ref[0, s], tag)
        comp = jnp.where(here, observed_ref[0, s] & 3, comp)
    inside = lane - start
    own = species_ref[...]

    for base in range(0, atoms, 128):
        cols = slice(base, base + 128)
        listed = neighbours_ref[:, cols]
        near = jnp.minimum(listed, struct_size - 1)
        index = near + (start[:, cols] - base)

        def pick(row):
            wide = jnp.broadcast_to(row, (slots, 128))
            return jnp.take_along_axis(wide, index, axis=1, mode="promise_in_bounds")

        shift_by = []
        for axis in range(3):
            mine = positions_ref[axis : axis + 1, cols]
            shift_by.append(pick(mine) - mine)
        distance_sq = shift_by[0] * shift_by[0]
        for axis in range(1, 3):
            distance_sq = distance_sq + shift_by[axis] * shift_by[axis]
        live = listed < struct_size
        radial = jnp.where(live, jnp.exp(-distance_sq / radial_width), 0.0)
        near_species = pick(own[:, cols].astype(jnp.float32))
        kind = comp[:, cols]
        along = jnp.where(kind == 1, shift_by[0], 0.0)
        along = jnp.where(kind == 2, shift_by[1], along)
        along = jnp.where(kind == 3, shift_by[2], along)
        moved = (near == tag[:, cols]).astype(jnp.float32) - (
            inside[:, cols] == tag[:, cols]
        ).astype(jnp.float32)
        slope = (-2.0 / radial_width) * radial * along * moved
        for k in range(slots):
            radial_ref[k, :, cols] = jnp.broadcast_to(radial[k : k + 1], (8, 128))
            slope_ref[k, :, cols] = jnp.broadcast_to(slope[k : k + 1], (8, 128))
            near_ref[k, :, cols] = jnp.broadcast_to(near_species[k : k + 1], (8, 128))

    scale_t = scale_ref[...].T
    shift_t = shift_ref[...].T
    for i in range(species_count):
        scale_cols[i] = jnp.broadcast_to(scale_t[:, i : i + 1], (channels, 128))
        shift_cols[i] = jnp.broadcast_to(shift_t[:, i : i + 1], (channels, 128))

    def embed(group, _):
        group_rows = pl.ds(pl.multiple_of(group * 8, 8), 8)
        scales = [scale_cols[i, group_rows, :] for i in range(species_count)]
        shifts = [shift_cols[i, group_rows, :] for i in range(species_count)]
        for base in range(0, atoms, 128):
            cols = slice(base, base + 128)
            total = jnp.zeros((8, 128), jnp.float32)
            moved = jnp.zeros((8, 128), jnp.float32)
            for k in range(slots):
                radial = radial_ref[k, :, cols]
                slope = slope_ref[k, :, cols]
                near = near_ref[k, :, cols]
                scale, shift = scales[-1], shifts[-1]
                for i in range(species_count - 1):
                    same = near == float(i)
                    scale = jnp.where(same, scales[i], scale)
                    shift = jnp.where(same, shifts[i], shift)
                scaled = radial * scale
                bent = jnp.tanh(scaled + shift)
                total = total + radial * bent
                moved = moved + slope * (bent + scaled * (1.0 - bent * bent))
            desc_ref[group_rows, cols] = total * (1.0 / slots)
            desc_ref[group_rows, slice(atoms + base, atoms + base + 128)] = moved * (
                1.0 / slots
            )
        return 0

    lax.fori_loop(0, channels // 8, embed, 0)

    first_bias = jnp.broadcast_to(first_bias_ref[...], (8, hidden)).T[:, :1]
    middle_bias = jnp.broadcast_to(middle_bias_ref[...], (8, hidden)).T[:, :1]
    energy_t = energy_ref[...].T
    lower = contract(first_weight_ref[...], desc_ref[...], 0, 0)
    first = jnp.tanh(lower[:, :atoms] + first_bias)
    first_moved = (1.0 - first * first) * lower[:, atoms:]
    upper = contract(middle_ref[...], jnp.concatenate([first, first_moved], axis=1), 0, 0)
    second = jnp.tanh(upper[:, :atoms] + middle_bias)
    moved = upper[:, atoms:]
    readout = jnp.broadcast_to(
        energy_t[:, species_count - 1 : species_count], (hidden, atoms)
    )
    for i in range(species_count - 1):
        readout = jnp.where(own == i, energy_t[:, i : i + 1], readout)
    gate = readout * (1.0 - second * second)
    mean = jnp.where(comp == 0, 1.0 / struct_size, 0.0)
    value = mean * jnp.sum(readout * second, axis=0, keepdims=True) - jnp.sum(
        gate * moved, axis=0, keepdims=True
    )
    bend = 2.0 * second * gate * moved + mean * gate

    struct_row = lax.broadcasted_iota(jnp.int32, (structs, atoms), 0)
    member = jnp.where(start == struct_row * struct_size, weighting, 0.0)
    struct_value = jnp.sum(member * value, axis=1, keepdims=True)
    left = jnp.concatenate([-first_moved[:rows], first[:rows]], axis=1)
    right = jnp.concatenate([gate, bend], axis=1)
    member_twice = jnp.concatenate([member, member], axis=1)
    spread = (left[:, None, :] * member_twice[None]).reshape(rows * structs, 2 * atoms)
    terms = contract(spread, right, 1, 1)
    for h in range(rows):
        place = AUX + (h % block_rows) * hidden
        out_ref[h // block_rows, :, place : place + hidden] = terms[
            h * structs : (h + 1) * structs
        ]
    row = lax.broadcasted_iota(jnp.int32, (structs, AUX), 0)
    column = lax.broadcasted_iota(jnp.int32, (structs, AUX), 1)
    observed = jnp.zeros((structs, AUX), jnp.int32)
    for s in range(structs):
        observed = jnp.where(row == s, observed_ref[0, s], observed)
    aux = jnp.where(
        column < OBS, (observed == column).astype(jnp.float32), struct_value
    )
    for b in range(blocks):
        out_ref[b, :, :AUX] = aux


def observe(
    blocks,
    order,
    weighting,
    positions,
    neighbours,
    atom_species,
    tagged_atom,
    observed_in,
    embed_scale,
    embed_shift,
    first_weight,
    first_bias,
    middle_weight,
    middle_bias,
    energy_weight,
):
    atoms = positions.shape[1]
    structs = tagged_atom.shape[0]
    slots = neighbours.shape[0]
    species_count, channels = embed_scale.shape
    vmem = pl.BlockSpec(memory_space=pltpu.VMEM)
    smem = pl.BlockSpec(memory_space=pltpu.SMEM)
    return pl.pallas_call(
        functools.partial(observe_kernel, weighting),
        out_shape=jax.ShapeDtypeStruct((blocks, structs, order + AUX), jnp.float32),
        in_specs=[smem, smem] + [vmem] * 10,
        out_specs=vmem,
        scratch_shapes=[
            pltpu.VMEM((slots, 8, atoms), jnp.float32),
            pltpu.VMEM((slots, 8, atoms), jnp.float32),
            pltpu.VMEM((slots, 8, atoms), jnp.float32),
            pltpu.VMEM((species_count, channels, 128), jnp.float32),
            pltpu.VMEM((species_count, channels, 128), jnp.float32),
            pltpu.VMEM((channels, 2 * atoms), jnp.float32),
        ],
    )(
        tagged_atom[None],
        observed_in[None],
        positions,
        neighbours,
        atom_species[None],
        embed_scale,
        embed_shift,
        first_weight,
        first_bias[None],
        middle_weight,
        middle_bias[None],
        energy_weight,
    )


MESH = pl.DeviceIdType.MESH


def exchange_kernel(
    group_count,
    block_count,
    terms_ref,
    cov_ref,
    product_ref,
    gram_ref,
    aux_ref,
    got,
    jac,
    cov_rows,
    total,
    gram_mine,
    gram_near,
    gram_sum,
    gram_far,
    cov_sem,
    own_sem,
    term_send,
    term_recv,
    jac_send,
    jac_recv,
    gram_send,
    gram_recv,
    far_send,
    far_recv,
    product_send,
    product_recv,
):
    group = lax.axis_index("dp")
    block = lax.axis_index("block")
    structs, width = terms_ref.shape[1:]
    obs_group = jac.shape[1]
    row_share = cov_ref.shape[0]
    piece = (width - AUX) // CHUNKS
    chunks = [(0, AUX + piece)]
    chunks += [(AUX + c * piece, piece) for c in range(1, CHUNKS)]
    group_peers = [(o, lax.rem(group + o, group_count)) for o in range(1, group_count)]
    block_peers = [(o, lax.rem(block + o, block_count)) for o in range(1, block_count)]

    cov_copy = pltpu.make_async_copy(cov_ref, cov_rows, cov_sem)
    cov_copy.start()
    own_copy = pltpu.make_async_copy(terms_ref.at[block], got.at[0], own_sem)
    own_copy.start()

    barrier = pltpu.get_barrier_semaphore()
    for _, peer in group_peers:
        pl.semaphore_signal(
            barrier, inc=1, device_id={"dp": peer}, device_id_type=MESH
        )
    for _, peer in block_peers:
        pl.semaphore_signal(
            barrier, inc=1, device_id={"block": peer}, device_id_type=MESH
        )
    pl.semaphore_wait(barrier, group_count + block_count - 2)

    def send(source, target, send_sem, recv_sem, device_id):
        copy = pltpu.make_async_remote_copy(
            src_ref=source,
            dst_ref=target,
            send_sem=send_sem,
            recv_sem=recv_sem,
            device_id=device_id,
            device_id_type=MESH,
        )
        copy.start()
        return copy

    term_copies = []
    for c, (base, size) in enumerate(chunks):
        cols = pl.ds(base, size)
        term_copies.append(
            [
                send(
                    terms_ref.at[peer, :, cols],
                    got.at[o, :, cols],
                    term_send.at[c, o - 1],
                    term_recv.at[c, o - 1],
                    {"block": peer},
                )
                for o, peer in block_peers
            ]
        )
    own_copy.wait()

    jac_copies = []
    for c, (base, size) in enumerate(chunks):
        cols = pl.ds(base, size)
        for copy in term_copies[c]:
            copy.wait_recv()
        chosen = got[:, :, :AUX].reshape(block_count * structs, AUX).T[:obs_group]
        pieces = got[:, :, cols].reshape(block_count * structs, size)
        jac[group, :, cols] = contract(chosen, pieces, 1, 0, exact_left=True)
        jac_copies.append(
            [
                send(
                    jac.at[group, :, cols],
                    jac.at[group, :, cols],
                    jac_send.at[c, o - 1],
                    jac_recv.at[c, o - 1],
                    {"dp": peer},
                )
                for o, peer in group_peers
            ]
        )

    cov_copy.wait()
    for c in range(CHUNKS):
        for copy in jac_copies[c]:
            copy.wait_recv()
        rows = jac[:, :, AUX + c * piece : AUX + (c + 1) * piece].reshape(OBS, piece)
        rows = jnp.concatenate([rows, jnp.zeros_like(rows)], axis=0)
        part = contract(cov_rows[:, c * piece : (c + 1) * piece], rows, 1, 1)
        total[...] = part if c == 0 else total[...] + part
    product = total[...].T
    product_ref[group] = product[:OBS]
    mine = jac[:, :, pl.ds(pl.multiple_of(AUX + group * row_share, 128), row_share)]
    gram = contract(mine.reshape(OBS, row_share), product, 1, 1)
    fold = OBS // 2
    gram_mine[...] = gram[:fold] + pltpu.roll(gram[fold:], 64, 1)
    gram_copies = [
        send(
            gram_mine,
            gram_near.at[o - 1],
            gram_send.at[o - 1],
            gram_recv.at[o - 1],
            {"dp": peer},
        )
        for o, peer in group_peers
    ]
    product_copies = [
        send(
            product_ref.at[group],
            product_ref.at[group],
            product_send.at[o - 1],
            product_recv.at[o - 1],
            {"dp": peer},
        )
        for o, peer in group_peers
    ]
    aux_ref[...] = jac[:, :, :AUX]
    summed = gram_mine[...]
    for i, copy in enumerate(gram_copies):
        copy.wait_recv()
        summed = summed + gram_near[i]
    gram_sum[...] = summed
    far_copies = [
        send(
            gram_sum,
            gram_far.at[o - 1],
            far_send.at[o - 1],
            far_recv.at[o - 1],
            {"block": peer},
        )
        for o, peer in block_peers
    ]
    for i, copy in enumerate(far_copies):
        copy.wait_recv()
        summed = summed + gram_far[i]
    gram_ref[:fold] = summed
    gram_ref[fold:] = pltpu.roll(summed, 64, 1)
    for copy in product_copies:
        copy.wait_recv()
    for copies in term_copies + jac_copies + [gram_copies, far_copies, product_copies]:
        for copy in copies:
            copy.wait_send()


def exchange(group_count, obs_group, terms, cov_rows):
    block_count, structs, width = terms.shape
    row_share, order = cov_rows.shape
    vmem = pl.BlockSpec(memory_space=pltpu.VMEM)
    fold = OBS // 2
    dma = pltpu.SemaphoreType.DMA
    near, far = group_count - 1, block_count - 1
    return pl.pallas_call(
        functools.partial(exchange_kernel, group_count, block_count),
        out_shape=(
            jax.ShapeDtypeStruct((group_count, OBS, row_share), jnp.float32),
            jax.ShapeDtypeStruct((OBS, 128), jnp.float32),
            jax.ShapeDtypeStruct((group_count, obs_group, AUX), jnp.float32),
        ),
        in_specs=[vmem, pl.BlockSpec(memory_space=pl.ANY)],
        out_specs=(vmem, vmem, vmem),
        scratch_shapes=[
            pltpu.VMEM((block_count, structs, width), jnp.float32),
            pltpu.VMEM((group_count, obs_group, width), jnp.float32),
            pltpu.VMEM((row_share, order), jnp.float32),
            pltpu.VMEM((row_share, 128), jnp.float32),
            pltpu.VMEM((fold, 128), jnp.float32),
            pltpu.VMEM((near, fold, 128), jnp.float32),
            pltpu.VMEM((fold, 128), jnp.float32),
            pltpu.VMEM((far, fold, 128), jnp.float32),
            dma,
            dma,
            dma((CHUNKS, far)),
            dma((CHUNKS, far)),
            dma((CHUNKS, near)),
            dma((CHUNKS, near)),
            dma((near,)),
            dma((near,)),
            dma((far,)),
            dma((far,)),
            dma((near,)),
            dma((near,)),
        ],
        compiler_params=pltpu.CompilerParams(collective_id=0, has_side_effects=True),
    )(terms, cov_rows)


def update_kernel(
    gram_ref,
    product_ref,
    aux_ref,
    targets_ref,
    noise_ref,
    middle_ref,
    cov_ref,
    weights_ref,
    new_cov_ref,
    gain_ref,
    cov_rows,
    cov_sem,
):
    step = pl.program_id(0)
    tile, order = new_cov_ref.shape
    row_share = product_ref.shape[2]
    hidden = middle_ref.shape[1]

    @pl.when(step == 0)
    def _():
        cov_copy = pltpu.make_async_copy(cov_ref, cov_rows, cov_sem)
        cov_copy.start()
        row = lax.broadcasted_iota(jnp.int32, (OBS, OBS), 0)
        column = lax.broadcasted_iota(jnp.int32, (OBS, OBS), 1)
        gram = gram_ref[...]
        pad = jnp.zeros((128 - OBS, 128), jnp.float32)
        flipped = jnp.concatenate([gram, pad], axis=0).T[:OBS]
        matrix = 0.5 * (gram + flipped)[:, :OBS]
        matrix = matrix + jnp.where(row == column, noise_ref[...], 0.0)
        for k in range(0, OBS, 2):
            upper = matrix[k : k + 1]
            lower = matrix[k + 1 : k + 2]
            cross = upper[:, k + 1 : k + 2]
            first_inverse = 1.0 / upper[:, k : k + 1]
            ratio = cross * first_inverse
            last = 1.0 / (lower[:, k + 1 : k + 2] - cross * ratio)
            mixed = -ratio * last
            first = first_inverse + ratio * ratio * last
            place = column[:1]
            upper_new = jnp.where(place == k, first, first * upper + mixed * lower)
            upper_new = jnp.where(place == k + 1, mixed, upper_new)
            lower_new = jnp.where(place == k, mixed, mixed * upper + last * lower)
            lower_new = jnp.where(place == k + 1, last, lower_new)
            left = jnp.where(row[:, :1] == k, -1.0, matrix[:, k : k + 1])
            left = jnp.where(row[:, :1] == k + 1, 0.0, left)
            right = jnp.where(row[:, :1] == k + 1, -1.0, matrix[:, k + 1 : k + 2])
            right = jnp.where(row[:, :1] == k, 0.0, right)
            kept = jnp.where(jnp.logical_or(row >> 1 == k // 2, column >> 1 == k // 2), 0.0, matrix)
            matrix = kept - left * upper_new - right * lower_new
        group = lax.axis_index("dp")
        gain = contract(product_ref[group], matrix, 0, 0)
        gain_ref[...] = gain
        predicted = jnp.sum(
            jnp.where(row == column, aux_ref[:, 128 - OBS :], 0.0), axis=0, keepdims=True
        )
        innovation = jnp.broadcast_to(targets_ref[...] - predicted, (8, OBS))
        moved = contract(innovation, gain, 1, 1)[:1]
        first = lax.axis_index("block") * order + group * row_share
        for i in range(row_share // 128):
            flat = first + i * 128
            line = middle_ref[pl.ds(flat // hidden, 1), :]
            window = line[:, :128]
            for j in range(1, hidden // 128):
                window = jnp.where(
                    lax.rem(flat, hidden) == j * 128,
                    line[:, j * 128 : (j + 1) * 128],
                    window,
                )
            here = slice(i * 128, (i + 1) * 128)
            weights_ref[:, here] = window + moved[:, here]
        cov_copy.wait()

    rows = pl.ds(pl.multiple_of(step * tile, tile), tile)
    gain = gain_ref[rows, :]
    for d in range(product_ref.shape[0]):
        cols = slice(d * row_share, (d + 1) * row_share)
        update = contract(gain, product_ref[d], 1, 0)
        new_cov_ref[:, cols] = (cov_rows[rows, cols] - update) * (1.0 / forgetting)


def update(gram, product, aux, targets, noise_level, middle_weight, cov_rows):
    row_share, order = cov_rows.shape
    tile = min(128, row_share)
    vmem = pl.BlockSpec(memory_space=pltpu.VMEM)
    cov_spec = pl.BlockSpec((tile, order), lambda i: (i, 0))
    return pl.pallas_call(
        update_kernel,
        grid=(row_share // tile,),
        out_shape=(
            jax.ShapeDtypeStruct((1, row_share), jnp.float32),
            jax.ShapeDtypeStruct((row_share, order), jnp.float32),
        ),
        in_specs=[vmem] * 6 + [pl.BlockSpec(memory_space=pl.ANY)],
        out_specs=(pl.BlockSpec((1, row_share), lambda i: (0, 0)), cov_spec),
        scratch_shapes=[
            pltpu.VMEM((row_share, OBS), jnp.float32),
            pltpu.VMEM((row_share, order), jnp.float32),
            pltpu.SemaphoreType.DMA,
        ],
    )(
        gram,
        product,
        aux.reshape(OBS, AUX),
        targets[None],
        noise_level[None],
        middle_weight,
        cov_rows,
    )


def local(
    positions,
    neighbours,
    atom_species,
    tagged_atom,
    observed_in,
    targets,
    noise_level,
    embed_scale,
    embed_shift,
    first_weight,
    first_bias,
    middle_weight,
    middle_bias,
    energy_weight,
    covariance,
):
    group_count = lax.axis_size("dp")
    block_count = lax.axis_size("block")
    block_order = covariance.shape[2]
    obs_group = OBS // group_count
    weighting = OBS / (tagged_atom.shape[0] * group_count * block_count)
    terms = observe(
        block_count,
        block_order,
        weighting,
        positions,
        neighbours,
        atom_species,
        tagged_atom,
        observed_in,
        embed_scale,
        embed_shift,
        first_weight,
        first_bias,
        middle_weight,
        middle_bias,
        energy_weight,
    )
    product, gram, aux = exchange(group_count, obs_group, terms, covariance[0])
    new_weights, new_rows = update(
        gram, product, aux, targets, noise_level, middle_weight, covariance[0]
    )
    return (new_weights, new_rows[None])


def solution(mesh):
    return jax.shard_map(
        local,
        mesh=mesh,
        in_specs=(
            P(None, ("dp", "block")),
            P(None, ("dp", "block")),
            P(("dp", "block")),
            P(("dp", "block")),
            P(("dp", "block")),
            P(),
            P(),
            P(),
            P(),
            P(),
            P(),
            P(),
            P(),
            P(),
            P("block", "dp", None),
        ),
        out_specs=(P("block", "dp"), P("block", "dp", None)),
        check_vma=False,
    )
```

```python
import functools

import jax
import jax.numpy as jnp
from jax import lax
from jax.experimental import pallas as pl
from jax.experimental.pallas import tpu as pltpu
from jax.sharding import PartitionSpec as P

OBS = 64
AUX = 128
CHUNKS = 4

radial_width = 4.0
forgetting = 0.98


def halves(value):
    high = value.astype(jnp.bfloat16)
    return high, (value - high.astype(jnp.float32)).astype(jnp.bfloat16)


def contract(left, right, left_dim, right_dim, exact_left=False):
    def one(a, b):
        return lax.dot_general(
            a,
            b,
            (((left_dim,), (right_dim,)), ((), ())),
            preferred_element_type=jnp.float32,
        )

    right_high, right_low = halves(right)
    left_high, left_low = halves(left)
    small = one(left_high, right_low)
    if not exact_left:
        small = small + one(left_low, right_high)
    return small + one(left_high, right_high)


def observe_kernel(
    weighting,
    tagged_ref,
    observed_ref,
    positions_ref,
    neighbours_ref,
    species_ref,
    scale_ref,
    shift_ref,
    first_weight_ref,
    first_bias_ref,
    middle_ref,
    middle_bias_ref,
    energy_ref,
    out_ref,
    radial_ref,
    slope_ref,
    near_ref,
    scale_cols,
    shift_cols,
    desc_ref,
):
    atoms = positions_ref.shape[1]
    structs = tagged_ref.shape[1]
    struct_size = atoms // structs
    slots = neighbours_ref.shape[0]
    species_count, channels = scale_ref.shape
    hidden = middle_ref.shape[1]
    blocks = out_ref.shape[0]
    order = out_ref.shape[2] - AUX
    block_rows = order // hidden
    rows = blocks * block_rows

    lane = lax.broadcasted_iota(jnp.int32, (1, atoms), 1)
    start = jnp.zeros_like(lane)
    tag = jnp.zeros_like(lane)
    comp = jnp.zeros_like(lane)
    for s in range(structs):
        here = jnp.logical_and(lane >= s * struct_size, lane < (s + 1) * struct_size)
        start = jnp.where(here, s * struct_size, start)
        tag = jnp.where(here, tagged_ref[0, s], tag)
        comp = jnp.where(here, observed_ref[0, s] & 3, comp)
    inside = lane - start
    own = species_ref[...]

    for base in range(0, atoms, 128):
        cols = slice(base, base + 128)
        listed = neighbours_ref[:, cols]
        near = jnp.minimum(listed, struct_size - 1)
        index = near + (start[:, cols] - base)

        def pick(row):
            wide = jnp.broadcast_to(row, (slots, 128))
            return jnp.take_along_axis(wide, index, axis=1, mode="promise_in_bounds")

        shift_by = []
        for axis in range(3):
            mine = positions_ref[axis : axis + 1, cols]
            shift_by.append(pick(mine) - mine)
        distance_sq = shift_by[0] * shift_by[0]
        for axis in range(1, 3):
            distance_sq = distance_sq + shift_by[axis] * shift_by[axis]
        live = listed < struct_size
        radial = jnp.where(live, jnp.exp(-distance_sq / radial_width), 0.0)
        near_species = pick(own[:, cols].astype(jnp.float32))
        kind = comp[:, cols]
        along = jnp.where(kind == 1, shift_by[0], 0.0)
        along = jnp.where(kind == 2, shift_by[1], along)
        along = jnp.where(kind == 3, shift_by[2], along)
        moved = (near == tag[:, cols]).astype(jnp.float32) - (
            inside[:, cols] == tag[:, cols]
        ).astype(jnp.float32)
        slope = (-2.0 / radial_width) * radial * along * moved
        for k in range(slots):
            radial_ref[k, :, cols] = jnp.broadcast_to(radial[k : k + 1], (8, 128))
            slope_ref[k, :, cols] = jnp.broadcast_to(slope[k : k + 1], (8, 128))
            near_ref[k, :, cols] = jnp.broadcast_to(near_species[k : k + 1], (8, 128))

    scale_t = scale_ref[...].T
    shift_t = shift_ref[...].T
    for i in range(species_count):
        scale_cols[i] = jnp.broadcast_to(scale_t[:, i : i + 1], (channels, 128))
        shift_cols[i] = jnp.broadcast_to(shift_t[:, i : i + 1], (channels, 128))

    def embed(group, _):
        group_rows = pl.ds(pl.multiple_of(group * 8, 8), 8)
        scales = [scale_cols[i, group_rows, :] for i in range(species_count)]
        shifts = [shift_cols[i, group_rows, :] for i in range(species_count)]
        for base in range(0, atoms, 128):
            cols = slice(base, base + 128)
            total = jnp.zeros((8, 128), jnp.float32)
            moved = jnp.zeros((8, 128), jnp.float32)
            for k in range(slots):
                radial = radial_ref[k, :, cols]
                slope = slope_ref[k, :, cols]
                near = near_ref[k, :, cols]
                scale, shift = scales[-1], shifts[-1]
                for i in range(species_count - 1):
                    same = near == float(i)
                    scale = jnp.where(same, scales[i], scale)
                    shift = jnp.where(same, shifts[i], shift)
                scaled = radial * scale
                bent = jnp.tanh(scaled + shift)
                total = total + radial * bent
                moved = moved + slope * (bent + scaled * (1.0 - bent * bent))
            desc_ref[group_rows, cols] = total * (1.0 / slots)
            desc_ref[group_rows, slice(atoms + base, atoms + base + 128)] = moved * (
                1.0 / slots
            )
        return 0

    lax.fori_loop(0, channels // 8, embed, 0)

    first_bias = jnp.broadcast_to(first_bias_ref[...], (8, hidden)).T[:, :1]
    middle_bias = jnp.broadcast_to(middle_bias_ref[...], (8, hidden)).T[:, :1]
    energy_t = energy_ref[...].T
    lower = contract(first_weight_ref[...], desc_ref[...], 0, 0)
    first = jnp.tanh(lower[:, :atoms] + first_bias)
    first_moved = (1.0 - first * first) * lower[:, atoms:]
    upper = contract(middle_ref[...], jnp.concatenate([first, first_moved], axis=1), 0, 0)
    second = jnp.tanh(upper[:, :atoms] + middle_bias)
    moved = upper[:, atoms:]
    readout = jnp.broadcast_to(
        energy_t[:, species_count - 1 : species_count], (hidden, atoms)
    )
    for i in range(species_count - 1):
        readout = jnp.where(own == i, energy_t[:, i : i + 1], readout)
    gate = readout * (1.0 - second * second)
    mean = jnp.where(comp == 0, 1.0 / struct_size, 0.0)
    value = mean * jnp.sum(readout * second, axis=0, keepdims=True) - jnp.sum(
        gate * moved, axis=0, keepdims=True
    )
    bend = 2.0 * second * gate * moved + mean * gate

    struct_row = lax.broadcasted_iota(jnp.int32, (structs, atoms), 0)
    member = jnp.where(start == struct_row * struct_size, weighting, 0.0)
    struct_value = jnp.sum(member * value, axis=1, keepdims=True)
    left = jnp.concatenate([-first_moved[:rows], first[:rows]], axis=1)
    right = jnp.concatenate([gate, bend], axis=1)
    member_twice = jnp.concatenate([member, member], axis=1)
    spread = (left[:, None, :] * member_twice[None]).reshape(rows * structs, 2 * atoms)
    terms = contract(spread, right, 1, 1)
    for h in range(rows):
        place = AUX + (h % block_rows) * hidden
        out_ref[h // block_rows, :, place : place + hidden] = terms[
            h * structs : (h + 1) * structs
        ]
    row = lax.broadcasted_iota(jnp.int32, (structs, AUX), 0)
    column = lax.broadcasted_iota(jnp.int32, (structs, AUX), 1)
    observed = jnp.zeros((structs, AUX), jnp.int32)
    for s in range(structs):
        observed = jnp.where(row == s, observed_ref[0, s], observed)
    aux = jnp.where(
        column < OBS, (observed == column).astype(jnp.float32), struct_value
    )
    for b in range(blocks):
        out_ref[b, :, :AUX] = aux


def observe(
    blocks,
    order,
    weighting,
    positions,
    neighbours,
    atom_species,
    tagged_atom,
    observed_in,
    embed_scale,
    embed_shift,
    first_weight,
    first_bias,
    middle_weight,
    middle_bias,
    energy_weight,
):
    atoms = positions.shape[1]
    structs = tagged_atom.shape[0]
    slots = neighbours.shape[0]
    species_count, channels = embed_scale.shape
    vmem = pl.BlockSpec(memory_space=pltpu.VMEM)
    smem = pl.BlockSpec(memory_space=pltpu.SMEM)
    return pl.pallas_call(
        functools.partial(observe_kernel, weighting),
        out_shape=jax.ShapeDtypeStruct((blocks, structs, order + AUX), jnp.float32),
        in_specs=[smem, smem] + [vmem] * 10,
        out_specs=vmem,
        scratch_shapes=[
            pltpu.VMEM((slots, 8, atoms), jnp.float32),
            pltpu.VMEM((slots, 8, atoms), jnp.float32),
            pltpu.VMEM((slots, 8, atoms), jnp.float32),
            pltpu.VMEM((species_count, channels, 128), jnp.float32),
            pltpu.VMEM((species_count, channels, 128), jnp.float32),
            pltpu.VMEM((channels, 2 * atoms), jnp.float32),
        ],
    )(
        tagged_atom[None],
        observed_in[None],
        positions,
        neighbours,
        atom_species[None],
        embed_scale,
        embed_shift,
        first_weight,
        first_bias[None],
        middle_weight,
        middle_bias[None],
        energy_weight,
    )


MESH = pl.DeviceIdType.MESH


def exchange_kernel(
    group_count,
    block_count,
    terms_ref,
    cov_ref,
    product_ref,
    gram_ref,
    aux_ref,
    got,
    jac,
    cov_rows,
    total,
    gram_mine,
    gram_near,
    gram_sum,
    gram_far,
    cov_sem,
    own_sem,
    term_send,
    term_recv,
    jac_send,
    jac_recv,
    gram_send,
    gram_recv,
    far_send,
    far_recv,
    product_send,
    product_recv,
):
    group = lax.axis_index("dp")
    block = lax.axis_index("block")
    structs, width = terms_ref.shape[1:]
    obs_group = jac.shape[1]
    row_share = cov_ref.shape[0]
    piece = (width - AUX) // CHUNKS
    chunks = [(0, AUX + piece)]
    chunks += [(AUX + c * piece, piece) for c in range(1, CHUNKS)]
    group_peers = [(o, lax.rem(group + o, group_count)) for o in range(1, group_count)]
    block_peers = [(o, lax.rem(block + o, block_count)) for o in range(1, block_count)]

    cov_copy = pltpu.make_async_copy(cov_ref, cov_rows, cov_sem)
    cov_copy.start()
    own_copy = pltpu.make_async_copy(terms_ref.at[block], got.at[0], own_sem)
    own_copy.start()

    barrier = pltpu.get_barrier_semaphore()
    for _, peer in group_peers:
        pl.semaphore_signal(
            barrier, inc=1, device_id={"dp": peer}, device_id_type=MESH
        )
    for _, peer in block_peers:
        pl.semaphore_signal(
            barrier, inc=1, device_id={"block": peer}, device_id_type=MESH
        )
    pl.semaphore_wait(barrier, group_count + block_count - 2)

    def send(source, target, send_sem, recv_sem, device_id):
        copy = pltpu.make_async_remote_copy(
            src_ref=source,
            dst_ref=target,
            send_sem=send_sem,
            recv_sem=recv_sem,
            device_id=device_id,
            device_id_type=MESH,
        )
        copy.start()
        return copy

    term_copies = []
    for c, (base, size) in enumerate(chunks):
        cols = pl.ds(base, size)
        term_copies.append(
            [
                send(
                    terms_ref.at[peer, :, cols],
                    got.at[o, :, cols],
                    term_send.at[c, o - 1],
                    term_recv.at[c, o - 1],
                    {"block": peer},
                )
                for o, peer in block_peers
            ]
        )
    own_copy.wait()

    jac_copies = []
    for c, (base, size) in enumerate(chunks):
        cols = pl.ds(base, size)
        for copy in term_copies[c]:
            copy.wait_recv()
        chosen = got[:, :, :AUX].reshape(block_count * structs, AUX).T[:obs_group]
        pieces = got[:, :, cols].reshape(block_count * structs, size)
        jac[group, :, cols] = contract(chosen, pieces, 1, 0, exact_left=True)
        jac_copies.append(
            [
                send(
                    jac.at[group, :, cols],
                    jac.at[group, :, cols],
                    jac_send.at[c, o - 1],
                    jac_recv.at[c, o - 1],
                    {"dp": peer},
                )
                for o, peer in group_peers
            ]
        )

    cov_copy.wait()
    for c in range(CHUNKS):
        for copy in jac_copies[c]:
            copy.wait_recv()
        rows = jac[:, :, AUX + c * piece : AUX + (c + 1) * piece].reshape(OBS, piece)
        rows = jnp.concatenate([rows, jnp.zeros_like(rows)], axis=0)
        part = contract(cov_rows[:, c * piece : (c + 1) * piece], rows, 1, 1)
        total[...] = part if c == 0 else total[...] + part
    product = total[...].T
    product_ref[group] = product[:OBS]
    mine = jac[:, :, pl.ds(pl.multiple_of(AUX + group * row_share, 128), row_share)]
    gram = contract(mine.reshape(OBS, row_share), product, 1, 1)
    fold = OBS // 2
    gram_mine[...] = gram[:fold] + pltpu.roll(gram[fold:], 64, 1)
    gram_copies = [
        send(
            gram_mine,
            gram_near.at[o - 1],
            gram_send.at[o - 1],
            gram_recv.at[o - 1],
            {"dp": peer},
        )
        for o, peer in group_peers
    ]
    product_copies = [
        send(
            product_ref.at[group],
            product_ref.at[group],
            product_send.at[o - 1],
            product_recv.at[o - 1],
            {"dp": peer},
        )
        for o, peer in group_peers
    ]
    aux_ref[...] = jac[:, :, :AUX]
    summed = gram_mine[...]
    for i, copy in enumerate(gram_copies):
        copy.wait_recv()
        summed = summed + gram_near[i]
    gram_sum[...] = summed
    far_copies = [
        send(
            gram_sum,
            gram_far.at[o - 1],
            far_send.at[o - 1],
            far_recv.at[o - 1],
            {"block": peer},
        )
        for o, peer in block_peers
    ]
    for i, copy in enumerate(far_copies):
        copy.wait_recv()
        summed = summed + gram_far[i]
    gram_ref[:fold] = summed
    gram_ref[fold:] = pltpu.roll(summed, 64, 1)
    for copy in product_copies:
        copy.wait_recv()
    for copies in term_copies + jac_copies + [gram_copies, far_copies, product_copies]:
        for copy in copies:
            copy.wait_send()


def exchange(group_count, obs_group, terms, cov_rows):
    block_count, structs, width = terms.shape
    row_share, order = cov_rows.shape
    vmem = pl.BlockSpec(memory_space=pltpu.VMEM)
    fold = OBS // 2
    dma = pltpu.SemaphoreType.DMA
    near, far = group_count - 1, block_count - 1
    return pl.pallas_call(
        functools.partial(exchange_kernel, group_count, block_count),
        out_shape=(
            jax.ShapeDtypeStruct((group_count, OBS, row_share), jnp.float32),
            jax.ShapeDtypeStruct((OBS, 128), jnp.float32),
            jax.ShapeDtypeStruct((group_count, obs_group, AUX), jnp.float32),
        ),
        in_specs=[vmem, pl.BlockSpec(memory_space=pl.ANY)],
        out_specs=(vmem, vmem, vmem),
        scratch_shapes=[
            pltpu.VMEM((block_count, structs, width), jnp.float32),
            pltpu.VMEM((group_count, obs_group, width), jnp.float32),
            pltpu.VMEM((row_share, order), jnp.float32),
            pltpu.VMEM((row_share, 128), jnp.float32),
            pltpu.VMEM((fold, 128), jnp.float32),
            pltpu.VMEM((near, fold, 128), jnp.float32),
            pltpu.VMEM((fold, 128), jnp.float32),
            pltpu.VMEM((far, fold, 128), jnp.float32),
            dma,
            dma,
            dma((CHUNKS, far)),
            dma((CHUNKS, far)),
            dma((CHUNKS, near)),
            dma((CHUNKS, near)),
            dma((near,)),
            dma((near,)),
            dma((far,)),
            dma((far,)),
            dma((near,)),
            dma((near,)),
        ],
        compiler_params=pltpu.CompilerParams(collective_id=0, has_side_effects=True),
    )(terms, cov_rows)


def update_kernel(
    gram_ref,
    product_ref,
    aux_ref,
    targets_ref,
    noise_ref,
    middle_ref,
    cov_ref,
    weights_ref,
    new_cov_ref,
    gain_ref,
    cov_rows,
    cov_sem,
):
    step = pl.program_id(0)
    tile, order = new_cov_ref.shape
    row_share = product_ref.shape[2]
    hidden = middle_ref.shape[1]

    @pl.when(step == 0)
    def _():
        cov_copy = pltpu.make_async_copy(cov_ref, cov_rows, cov_sem)
        cov_copy.start()
        row = lax.broadcasted_iota(jnp.int32, (OBS, OBS), 0)
        column = lax.broadcasted_iota(jnp.int32, (OBS, OBS), 1)
        gram = gram_ref[...]
        pad = jnp.zeros((128 - OBS, 128), jnp.float32)
        flipped = jnp.concatenate([gram, pad], axis=0).T[:OBS]
        matrix = 0.5 * (gram + flipped)[:, :OBS]
        matrix = matrix + jnp.where(row == column, noise_ref[...], 0.0)
        for k in range(OBS):
            pivot = 1.0 / matrix[k : k + 1, k : k + 1]
            scaled = jnp.where(column[:1] == k, pivot, matrix[k : k + 1] * pivot)
            side = jnp.where(row[:, :1] == k, -1.0, matrix[:, k : k + 1])
            kept = jnp.where(jnp.logical_or(row == k, column == k), 0.0, matrix)
            matrix = kept - side * scaled
        group = lax.axis_index("dp")
        gain = contract(product_ref[group], matrix, 0, 0)
        gain_ref[...] = gain
        predicted = jnp.sum(
            jnp.where(row == column, aux_ref[:, 128 - OBS :], 0.0), axis=0, keepdims=True
        )
        innovation = jnp.broadcast_to(targets_ref[...] - predicted, (8, OBS))
        moved = contract(innovation, gain, 1, 1)[:1]
        first = lax.axis_index("block") * order + group * row_share
        for i in range(row_share // 128):
            flat = first + i * 128
            line = middle_ref[pl.ds(flat // hidden, 1), :]
            window = line[:, :128]
            for j in range(1, hidden // 128):
                window = jnp.where(
                    lax.rem(flat, hidden) == j * 128,
                    line[:, j * 128 : (j + 1) * 128],
                    window,
                )
            here = slice(i * 128, (i + 1) * 128)
            weights_ref[:, here] = window + moved[:, here]
        cov_copy.wait()

    rows = pl.ds(pl.multiple_of(step * tile, tile), tile)
    gain = gain_ref[rows, :]
    for d in range(product_ref.shape[0]):
        cols = slice(d * row_share, (d + 1) * row_share)
        update = contract(gain, product_ref[d], 1, 0)
        new_cov_ref[:, cols] = (cov_rows[rows, cols] - update) * (1.0 / forgetting)


def update(gram, product, aux, targets, noise_level, middle_weight, cov_rows):
    row_share, order = cov_rows.shape
    tile = min(128, row_share)
    vmem = pl.BlockSpec(memory_space=pltpu.VMEM)
    cov_spec = pl.BlockSpec((tile, order), lambda i: (i, 0))
    return pl.pallas_call(
        update_kernel,
        grid=(row_share // tile,),
        out_shape=(
            jax.ShapeDtypeStruct((1, row_share), jnp.float32),
            jax.ShapeDtypeStruct((row_share, order), jnp.float32),
        ),
        in_specs=[vmem] * 6 + [pl.BlockSpec(memory_space=pl.ANY)],
        out_specs=(pl.BlockSpec((1, row_share), lambda i: (0, 0)), cov_spec),
        scratch_shapes=[
            pltpu.VMEM((row_share, OBS), jnp.float32),
            pltpu.VMEM((row_share, order), jnp.float32),
            pltpu.SemaphoreType.DMA,
        ],
    )(
        gram,
        product,
        aux.reshape(OBS, AUX),
        targets[None],
        noise_level[None],
        middle_weight,
        cov_rows,
    )


def local(
    positions,
    neighbours,
    atom_species,
    tagged_atom,
    observed_in,
    targets,
    noise_level,
    embed_scale,
    embed_shift,
    first_weight,
    first_bias,
    middle_weight,
    middle_bias,
    energy_weight,
    covariance,
):
    group_count = lax.axis_size("dp")
    block_count = lax.axis_size("block")
    block_order = covariance.shape[2]
    obs_group = OBS // group_count
    weighting = OBS / (tagged_atom.shape[0] * group_count * block_count)
    terms = observe(
        block_count,
        block_order,
        weighting,
        positions,
        neighbours,
        atom_species,
        tagged_atom,
        observed_in,
        embed_scale,
        embed_shift,
        first_weight,
        first_bias,
        middle_weight,
        middle_bias,
        energy_weight,
    )
    product, gram, aux = exchange(group_count, obs_group, terms, covariance[0])
    new_weights, new_rows = update(
        gram, product, aux, targets, noise_level, middle_weight, covariance[0]
    )
    return (new_weights, new_rows[None])


def solution(mesh):
    return jax.shard_map(
        local,
        mesh=mesh,
        in_specs=(
            P(None, ("dp", "block")),
            P(None, ("dp", "block")),
            P(("dp", "block")),
            P(("dp", "block")),
            P(("dp", "block")),
            P(),
            P(),
            P(),
            P(),
            P(),
            P(),
            P(),
            P(),
            P(),
            P("block", "dp", None),
        ),
        out_specs=(P("block", "dp"), P("block", "dp", None)),
        check_vma=False,
    )
```
